32 devices in a mesh: gx: 8 (over z, core), gy: 4 (over y, x).
Axes of the slice: x: 2, y: 2, z: 4, core: 2. Of those that a mesh axis runs over, the one named last changes fastest.
Arguments:
- grid_field: bfloat16 [1, 20, 2048, 2048], P(None, None, 'gx', 'gy'), may hold values from -8 to 8
- spectral_weight: float32 [2, 2, 20, 20, 2048], P(None, None, None, None, ('gx', 'gy')), may hold values from -1 to 1
- conv_near: bfloat16 [2, 20, 180], replicated, may hold values from -0.4375 to 0.4375
- conv_far: bfloat16 [2, 20, 500], replicated, may hold values from -0.25 to 0.25
- mix_logits: float32 [2, 3], replicated, may hold values from -1 to 1
- channel_bias: float32 [2, 20], replicated, may hold values from -3 to 3
Outputs:
- result_field: bfloat16 [1, 20, 2048, 2048], P(None, None, 'gx', 'gy')
The draws below stay inside these ranges and needn't reach their ends.
All inputs are finite; a program needn't handle non-finite values.
Results may differ from the reference program's by a relative error of at most 0.004.
Values may be sent and summed in bfloat16 or wider, within the bound.
A program may use at most 448 MiB of HBM per device.

```python
import math
import jax
import jax.numpy as jnp
from jax import lax

NX = 2048
NY = 2048
C = 20
MX = 32
MY = 32
LAYERS = 2
PLANES = 1
KX = 64
MODES = 2048


def wave_profile(sub_key, length, highest_mode):
    sub_keys = jax.random.split(sub_key, 2)
    frequency = jnp.arange(highest_mode, dtype=jnp.int32)
    amplitude = jax.random.normal(sub_keys[0], (PLANES, C, highest_mode, 1), jnp.float32) * math.sqrt(2.0 / highest_mode)
    phases = jax.random.uniform(sub_keys[1], (PLANES, C, highest_mode, 1), jnp.float32, 0.0, 2.0 * math.pi)
    positions = jnp.arange(length, dtype=jnp.int32)
    angle_grid = (frequency[:, None] * positions[None, :] % length).astype(jnp.float32) * (2.0 * math.pi / length)
    return jnp.sum(amplitude * jnp.cos(angle_grid[None, None, :, :] + phases), axis=2)


def draw_grid_field(key, part):
    noise_key, first_key, second_key = jax.random.split(jax.random.fold_in(key, 17), 3)
    roughness = jax.random.normal(noise_key, (PLANES, C, NX, NY), jnp.float32)
    profile_rows = wave_profile(first_key, NX, MX)
    profile_cols = wave_profile(second_key, NY, MY)
    smooth = profile_rows[:, :, :, None] * profile_cols[:, :, None, :]
    return jnp.clip(roughness + smooth, -8.0, 8.0).astype(jnp.bfloat16)


def level_of(stream_key, shape, cuts, low, largest):
    factor_of = 1.0
    for dim, shards_of in cuts:
        steps = jax.random.uniform(jax.random.fold_in(jax.random.fold_in(stream_key, 6), dim), (shards_of,), jnp.float32, low / len(cuts), largest / len(cuts))
        factor_of = factor_of * jnp.repeat(jnp.exp(steps), shape[dim] // shards_of).reshape((-1,) + (1,) * (len(shape) - 1 - dim))
    return factor_of


def scatter_about(rng, extent, deviation, reach, pieces=(), kind=jnp.bfloat16):
    values = jax.random.normal(rng, extent, jnp.float32) * deviation
    if len(pieces) > 0:
        values = level_of(rng, extent, pieces, -0.22, 0.18) * values
    return jnp.clip(values, min=-reach, max=reach).astype(kind)


def setup_inputs(seed: int = 0) -> dict:
    streams_of = jax.random.split(jax.random.key(seed), 7)
    grid_field = draw_grid_field(jax.random.fold_in(streams_of[6], 71), 0)
    spectral_weight = scatter_about(streams_of[1], (LAYERS, 2, C, C, MODES), (2 * C) ** -0.5, 1.0, ((4, 32),), jnp.float32)
    conv_near = scatter_about(streams_of[2], (LAYERS, C, 9 * C), (9 * C) ** -0.5, 0.4375)
    conv_far = scatter_about(streams_of[3], (LAYERS, C, 25 * C), (25 * C) ** -0.5, 0.25)
    mix_logits = jnp.clip(jax.random.uniform(streams_of[4], (LAYERS, 3), jnp.float32, -1.0, 1.0), -1.0, 1.0)
    channel_bias = scatter_about(streams_of[5], (LAYERS, C), 0.5, 3.0, (), jnp.float32)
    return {"grid_field": grid_field, "spectral_weight": spectral_weight, "conv_near": conv_near, "conv_far": conv_far, "mix_logits": mix_logits, "channel_bias": channel_bias}


full_turn = 2.0 * math.pi
highest = lax.Precision.HIGHEST


def forward_table(positions):
    col_modes = jnp.arange(MY, dtype=jnp.int32)
    phases = ((positions[:, None] * col_modes[None, :]) % NY).astype(jnp.float32) * (full_turn / NY)
    return jnp.concatenate([jnp.cos(phases), -jnp.sin(phases)], axis=1).astype(jnp.bfloat16)


def row_tables(positions):
    lower = jnp.arange(MX, dtype=jnp.int32)
    row_modes = jnp.concatenate([lower, lower + (NX - MX)])
    phases = ((positions[:, None] * row_modes[None, :]) % NX).astype(jnp.float32) * (full_turn / NX)
    return jnp.cos(phases), jnp.sin(phases)


def inverse_table(positions):
    col_modes = jnp.arange(MY, dtype=jnp.int32)
    col_weight = jnp.where(col_modes == 0, 1.0, 2.0).astype(jnp.float32) / (NX * NY)
    phases = ((col_modes[:, None] * positions[None, :]) % NY).astype(jnp.float32) * (full_turn / NY)
    return jnp.concatenate([jnp.cos(phases) * col_weight[:, None], -jnp.sin(phases) * col_weight[:, None]], axis=0)


def block_height():
    height = min(NX, 128)
    while NX % height != 0:
        height = height - 1
    return height


def mixed_spectrum(plane_field, weight_pair, forward_cols, cosine_rows, sine_rows):
    channels = plane_field.shape[0]
    line_sums = jnp.dot(plane_field.reshape(channels * NX, NY), forward_cols, preferred_element_type=jnp.float32)
    line_sums = line_sums.reshape(channels, NX, 2 * MY)
    real_lines = line_sums[..., :MY]
    imaginary_lines = line_sums[..., MY:]

    def contract_rows(operand, lookup):
        return jnp.einsum("cxk,xj->cjk", operand, lookup, precision=highest)

    real_spec = (contract_rows(real_lines, cosine_rows) + contract_rows(imaginary_lines, sine_rows)).reshape(channels, MODES)
    imaginary_spec = (contract_rows(imaginary_lines, cosine_rows) - contract_rows(real_lines, sine_rows)).reshape(channels, MODES)

    def mix_modes(spectrum, weights):
        return jnp.einsum("cm,com->om", spectrum, weights, precision=highest)

    real_mixed = mix_modes(real_spec, weight_pair[0]) - mix_modes(imaginary_spec, weight_pair[1])
    imaginary_mixed = mix_modes(imaginary_spec, weight_pair[0]) + mix_modes(real_spec, weight_pair[1])
    return real_mixed.reshape(channels, KX, MY), imaginary_mixed.reshape(channels, KX, MY)


def conv_block(padded_rows, tap_weights, dilation, side_taps, height):
    channels = padded_rows.shape[0]
    accumulated = jnp.zeros((channels, height * NY), jnp.float32)
    for tap_index in range(side_taps * side_taps):
        shift_row = (tap_index // side_taps - side_taps // 2) * dilation
        shift_col = (tap_index % side_taps - side_taps // 2) * dilation
        piece = padded_rows[:, 4 + shift_row:4 + shift_row + height, 4 + shift_col:4 + shift_col + NY]
        piece = piece.astype(jnp.float32).reshape(channels, height * NY)
        weights_tap = tap_weights[:, tap_index * channels:(tap_index + 1) * channels].astype(jnp.float32)
        accumulated = accumulated + jnp.dot(weights_tap, piece, precision=highest)
    return accumulated.reshape(channels, height, NY)


def reference(grid_field, spectral_weight, conv_near, conv_far, mix_logits, channel_bias):
    row_positions = jnp.arange(NX, dtype=jnp.int32)
    col_positions = jnp.arange(NY, dtype=jnp.int32)
    cosine_rows, sine_rows = row_tables(row_positions)
    forward_cols = forward_table(col_positions)
    inverse_cols = inverse_table(col_positions)
    height = block_height()
    block_starts = jnp.arange(NX // height, dtype=jnp.int32) * height

    def per_plane(plane_field):
        channels = plane_field.shape[0]
        for layer_index in range(LAYERS):
            real_mixed, imaginary_mixed = mixed_spectrum(plane_field, spectral_weight[layer_index], forward_cols, cosine_rows, sine_rows)
            padded = jnp.pad(plane_field, ((0, 0), (4, 4), (4, 4)), mode="wrap")
            exponents = jnp.exp(mix_logits[layer_index])
            mixture = exponents / jnp.sum(exponents)
            bias_column = channel_bias[layer_index][:, None, None]
            near_weights = conv_near[layer_index]
            far_weights = conv_far[layer_index]

            def per_block(start):
                cos_block = lax.dynamic_slice_in_dim(cosine_rows, start, height, 0)
                sin_block = lax.dynamic_slice_in_dim(sine_rows, start, height, 0)

                def expand_rows(spectrum, lookup):
                    return jnp.einsum("cjk,xj->cxk", spectrum, lookup, precision=highest)

                real_rows = expand_rows(real_mixed, cos_block) - expand_rows(imaginary_mixed, sin_block)
                imaginary_rows = expand_rows(real_mixed, sin_block) + expand_rows(imaginary_mixed, cos_block)
                stacked = jnp.concatenate([real_rows, imaginary_rows], axis=-1).reshape(channels * height, 2 * MY)
                spectral = jnp.dot(stacked, inverse_cols, precision=highest).reshape(channels, height, NY)
                padded_rows = lax.dynamic_slice_in_dim(padded, start, height + 8, 1)
                near_term = conv_block(padded_rows, near_weights, 1, 3, height)
                far_term = conv_block(padded_rows, far_weights, 2, 5, height)
                summed = mixture[0] * spectral + mixture[1] * near_term + mixture[2] * far_term + bias_column
                return jax.nn.gelu(summed, approximate=False).astype(jnp.bfloat16)

            blocks = lax.map(per_block, block_starts)
            plane_field = jnp.transpose(blocks, (1, 0, 2, 3)).reshape(channels, NX, NY)
        return plane_field

    return lax.map(per_plane, grid_field)
```

```python
import functools
import math

import jax
import jax.numpy as jnp
from jax import lax
from jax.experimental import pallas as pl
from jax.experimental.pallas import tpu as pltpu
from jax.sharding import PartitionSpec as P

full_turn = 2.0 * math.pi
MESH = pl.DeviceIdType.MESH
MODES_Y = 32
GROUP = 16
LANES = 128
NEAR = (-1, 0, 1)
FAR = (-4, -2, 0, 2, 4)
f32 = jnp.float32
bf16 = jnp.bfloat16


def split_bf16(value):
    high = value.astype(bf16)
    low = (value - high.astype(f32)).astype(bf16)
    return high, low


def prep_kernel(near_ref, far_ref, near_out, far_out):
    channels = near_ref.shape[1]
    pair = 2 * channels
    rows, depth = 4 * pair, 6 * pair

    def spread(taps_ref, out_ref, side, tap_of):
        taps = taps_ref[0]
        count = taps.shape[1]
        replicate = (
            lax.broadcasted_iota(jnp.int32, (rows, channels), 0) % channels
            == lax.broadcasted_iota(jnp.int32, (rows, channels), 1)
        ).astype(bf16)
        tall = jnp.dot(replicate, taps, preferred_element_type=f32).astype(bf16)
        source = lax.broadcasted_iota(jnp.int32, (count, depth), 0)
        target = lax.broadcasted_iota(jnp.int32, (count, depth), 1)
        same = source % channels == target % channels
        tap = source // channels
        out_at = lax.broadcasted_iota(jnp.int32, (rows, depth), 0)
        in_at = lax.broadcasted_iota(jnp.int32, (rows, depth), 1)
        wanted = tap_of(out_at // channels, in_at // channels)
        pieces = []
        for column in range(side):
            total = jnp.zeros((rows, depth), f32)
            for row in range(side):
                pick = (same & (tap == row * side + column)).astype(bf16)
                term = jnp.dot(tall, pick, preferred_element_type=f32)
                total = jnp.where(wanted == row, term, total)
            pieces.append(total)
        out_ref[0] = jnp.concatenate(pieces, axis=1).astype(bf16)

    def far_tap(out_row, in_row):
        return in_row - out_row

    def near_tap(out_row, in_row):
        out_pair, out_low = out_row // 2, out_row % 2
        out_at = 4 * (out_pair % 2) + 2 * out_low + out_pair // 2
        in_pair, in_low = in_row // 2, in_row % 2
        odd = 4 * (in_pair // 2 - 1) + 1 + 2 * in_low
        even = 4 * (in_pair // 2) + 2 * in_low
        in_at = jnp.where(in_pair % 2 == 0, odd, even)
        return in_at - out_at + 1

    spread(near_ref, near_out, 3, near_tap)
    spread(far_ref, far_out, 5, far_tap)


def prep_call(near, far):
    layers, channels, _ = near.shape
    rows, depth = 8 * channels, 12 * channels
    block = lambda shape: pl.BlockSpec((1,) + shape[1:], lambda i: (i, 0, 0))
    near_shape = (layers, rows, 3 * depth)
    far_shape = (layers, rows, 5 * depth)
    return pl.pallas_call(
        prep_kernel,
        grid=(layers,),
        name="prep",
        in_specs=[block(near.shape), block(far.shape)],
        out_specs=[block(near_shape), block(far_shape)],
        out_shape=[
            jax.ShapeDtypeStruct(near_shape, bf16),
            jax.ShapeDtypeStruct(far_shape, bf16),
        ],
    )(near, far)


def main_kernel(
    u_ref, sw_ref, near_ref, far_ref, order_ref, back_ref, fwd_ref, ftab_ref, itab_ref, inv_ref,
    bias_ref, mix_ref, out_ref,
    nst, fst, conv, lhs, lines, carry, pack, packs, edges, hcol, hrow,
    sendbuf, recv, mixed, gath,
    halo_send, halo_recv, a2a_send, a2a_recv, gat_send, gat_recv,
    *, sizes, first_part,
):
    gx, gy = sizes
    devices = gx * gy
    layers = sw_ref.shape[0]
    channels, local_rows, cols = u_ref.shape
    pair = 2 * channels
    half = 4 * pair
    whole = 2 * half
    groups = local_rows // GROUP
    wide = cols + 2 * LANES
    slot = mixed.shape[1]
    blocks = sendbuf.shape[1] // slot
    sharers = devices // blocks
    per_device = 2 * MODES_Y
    my_x, my_y = lax.axis_index("gx"), lax.axis_index("gy")
    me = my_x * gy + my_y

    def place(index):
        return (index // gy, index % gy)

    barrier = pltpu.get_barrier_semaphore()

    @pl.loop(1, devices)
    def _(k):
        pl.semaphore_signal(
            barrier, inc=1, device_id=place((me + k) % devices), device_id_type=MESH
        )

    def store_rows(g, even, odd, start):
        width = even.shape[1]
        at = slice(start, start + width)
        old_even, old_odd = carry[0, :, at], carry[1, :, at]
        q = [(even[i * pair : (i + 1) * pair], odd[i * pair : (i + 1) * pair]) for i in range(4)]
        near_rows = [old_odd]
        for i in range(4):
            near_rows.append(q[i][0])
            if i < 3:
                near_rows.append(q[i][1])
        nst[pl.ds(pl.multiple_of(g * whole, whole), whole), at] = jnp.concatenate(
            near_rows, axis=0
        ).astype(bf16)
        row = pl.ds(pl.multiple_of(g * half, half), half)
        fst[0, row, at] = jnp.concatenate([old_even, even[: 3 * pair]], axis=0).astype(bf16)
        fst[1, row, at] = jnp.concatenate([old_odd, odd[: 3 * pair]], axis=0).astype(bf16)
        carry[0, :, at] = q[3][0]
        carry[1, :, at] = q[3][1]

    lane = lax.broadcasted_iota(jnp.int32, (half, LANES), 1)

    def ingest(g, value, layer):
        even, odd = value[:half], value[half:]
        store_rows(g, even, odd, LANES)
        lines[pl.ds(pl.multiple_of(g * whole, whole), whole), :] = jnp.dot(
            value.astype(bf16), fwd_ref[...], preferred_element_type=f32
        )
        for p, part in enumerate((even, odd)):
            k = 2 * g + p
            mine = lane // 4 == k
            left = pltpu.roll(part[:, :LANES], 4 * k, 1)
            right = pltpu.roll(part[:, cols - LANES :], (4 * k + 4) % LANES, 1)
            pack[0] = jnp.where(mine, left, pack[0])
            pack[1] = jnp.where(mine, right, pack[1])

        @pl.when(g == 0)
        def _():
            edges[layer, 0] = jnp.concatenate([even[:pair], odd[:pair]], axis=0).astype(bf16)

        @pl.when(g == groups - 1)
        def _():
            edges[layer, 1] = jnp.concatenate(
                [even[3 * pair :], odd[3 * pair :]], axis=0
            ).astype(bf16)

    carry[...] = jnp.zeros_like(carry)
    pack[...] = jnp.zeros_like(pack)

    @pl.loop(0, groups)
    def _(g):
        slab = u_ref[:, pl.ds(pl.multiple_of(g * GROUP, GROUP), GROUP), :]
        value = jnp.dot(
            order_ref[...], slab.reshape(whole, cols), preferred_element_type=f32
        )
        ingest(g, value, 0)

    pl.semaphore_wait(barrier, devices - 1)

    up, down = (my_x + gx - 1) % gx, (my_x + 1) % gx
    left, right = (my_y + gy - 1) % gy, (my_y + 1) % gy
    last = cols - LANES

    def halo_copies(layer):
        def copy(i, src, dst, target):
            return pltpu.make_async_remote_copy(
                src_ref=src, dst_ref=dst, send_sem=halo_send.at[layer, i],
                recv_sem=halo_recv.at[layer, i], device_id=target, device_id_type=MESH,
            )

        top, bottom = edges.at[layer, 0], edges.at[layer, 1]
        above, below = hrow.at[layer, 0], hrow.at[layer, 1]
        head, mid, tail = slice(0, LANES), slice(LANES, LANES + cols), slice(LANES + cols, wide)
        return [
            copy(0, packs.at[layer, 0], hcol.at[layer, 1], (my_x, left)),
            copy(1, packs.at[layer, 1], hcol.at[layer, 0], (my_x, right)),
            copy(2, top, below.at[:, mid], (up, my_y)),
            copy(3, bottom, above.at[:, mid], (down, my_y)),
            copy(4, top.at[:, :LANES], below.at[:, tail], (up, left)),
            copy(5, bottom.at[:, :LANES], above.at[:, tail], (down, left)),
            copy(6, top.at[:, last:], below.at[:, head], (up, right)),
            copy(7, bottom.at[:, last:], above.at[:, head], (down, right)),
        ]

    def a2a_copy(layer, k):
        target = (me + k) % devices
        return pltpu.make_async_remote_copy(
            src_ref=sendbuf.at[layer, pl.ds(target // sharers * slot, slot)],
            dst_ref=recv.at[layer, k - 1],
            send_sem=a2a_send.at[layer, k - 1],
            recv_sem=a2a_recv.at[layer, k - 1],
            device_id=place(target),
            device_id_type=MESH,
        )

    def gather_copy(layer, k):
        return pltpu.make_async_remote_copy(
            src_ref=mixed.at[layer],
            dst_ref=gath.at[layer, pl.ds(me * slot, slot)],
            send_sem=gat_send.at[layer, k - 1],
            recv_sem=gat_recv.at[layer, k - 1],
            device_id=place((me + k) % devices),
            device_id_type=MESH,
        )

    modes_x = ftab_ref.shape[0] // 2
    share_rows = modes_x // blocks
    share = sw_ref.shape[-1]

    def turned(value):
        at = lax.broadcasted_iota(jnp.int32, value.shape, 1)
        return jnp.where(
            (at // MODES_Y) % 2 == 1,
            pltpu.roll(value, MODES_Y, 1),
            -pltpu.roll(value, LANES - MODES_Y, 1),
        )

    def row_transform(layer):
        @pl.loop(0, channels)
        def _(c):
            high, low = split_bf16(lines[pl.ds(c, local_rows, stride=channels), :])
            both = jnp.dot(
                ftab_ref[...],
                jnp.concatenate([high, low, high], axis=0),
                preferred_element_type=f32,
            )
            total = both[:modes_x] + pltpu.roll(both[modes_x:], per_device, 1)
            if share_rows == 2:
                at = lax.broadcasted_iota(jnp.int32, (blocks, LANES), 1)
                block = jnp.where(
                    at < per_device, total[:blocks], pltpu.roll(total[blocks:], per_device, 1)
                )
            else:
                block = total
            sendbuf[layer, pl.ds(c, blocks, stride=slot), :] = block

    def mix_modes(layer):
        own = sendbuf[layer, pl.ds(pl.multiple_of(me // sharers * slot, 8), slot), :]

        @pl.loop(1, devices)
        def _(k):
            a2a_copy(layer, k).wait_recv()

        own = own + jnp.sum(recv[layer], axis=0)
        crossed = turned(own)
        scale = mix_ref[layer, 0]

        def spread(part):
            if share_rows == 1:
                tiled = jnp.concatenate([part] * (LANES // share), axis=1)
                at = lax.broadcasted_iota(jnp.int32, tiled.shape, 1) // share
                return jnp.where(at % sharers == me % sharers, tiled, 0.0)
            pieces = []
            for j in range(share_rows):
                piece = part[:, j * MODES_Y : (j + 1) * MODES_Y]
                pieces += [piece, piece]
            return jnp.concatenate(pieces, axis=1)

        total = jnp.zeros((channels, LANES), f32)
        for c in range(channels):
            total = total + spread(sw_ref[layer, 0, c]) * own[c : c + 1]
            total = total + spread(sw_ref[layer, 1, c]) * crossed[c : c + 1]
        total = total * scale
        mixed[layer, :channels, :] = total
        gath[layer, pl.ds(pl.multiple_of(me * slot, 8), channels), :] = total

        @pl.loop(1, devices)
        def _(k):
            gather_copy(layer, k).start()

    def inverse_rows(layer):
        @pl.loop(1, devices)
        def _(k):
            gather_copy(layer, k).wait_recv()

        @pl.loop(0, channels)
        def _(o):
            block = gath[layer, pl.ds(o, blocks, stride=slot * sharers), :]
            for i in range(1, sharers):
                block = block + gath[layer, pl.ds(i * slot + o, blocks, stride=slot * sharers), :]
            cross = turned(block)
            if share_rows == 2:
                stack = [block, pltpu.roll(block, per_device, 1)]
                stack += [cross, pltpu.roll(cross, per_device, 1)]
            else:
                stack = [block, cross]
            high, low = split_bf16(jnp.concatenate(stack, axis=0))
            lhs[pl.ds(o, local_rows, stride=channels), :] = jnp.dot(
                itab_ref[...],
                jnp.concatenate([high, low, high], axis=0),
                preferred_element_type=f32,
            )

    def conv_group(layer, g):
        near_w, far_w = near_ref[layer], far_ref[layer]
        depth = 6 * pair

        def window(rows, shifts):
            return jnp.concatenate([rows[:, LANES + d : LANES + d + cols] for d in shifts], axis=0)

        near = []
        for h in range(2):
            rows = nst[pl.ds(pl.multiple_of(g * whole, whole) + h * half, depth), :]
            near.append(jnp.dot(near_w, window(rows, NEAR), preferred_element_type=f32))
        parts = []
        for p in range(2):
            rows = fst[p, pl.ds(pl.multiple_of(g * half, half), depth), :]
            far = jnp.dot(far_w, window(rows, FAR), preferred_element_type=f32)
            side = slice(p * 2 * pair, (p + 1) * 2 * pair)
            close = jnp.concatenate([near[0][side], near[1][side]], axis=0)
            total = mix_ref[layer, 1] * close + mix_ref[layer, 2] * far + bias_ref[layer]
            parts.append(total)
        conv[pl.ds(pl.multiple_of(g * whole, whole), whole), :] = jnp.concatenate(parts, axis=0)

    def finish_group(layer, g):
        at = pl.ds(pl.multiple_of(g * whole, whole), whole)
        high, low = split_bf16(lhs[at, :per_device])
        spectral = jnp.dot(
            jnp.concatenate([high, low, high], axis=1), inv_ref[...], preferred_element_type=f32
        )
        value = conv[at, :] + spectral
        value = (value * 0.5 * (1.0 + lax.erf(value * (0.5**0.5)))).astype(bf16)
        if layer + 1 < layers:
            ingest(g, value.astype(f32), layer + 1)
        else:
            natural = jnp.dot(back_ref[...], value, preferred_element_type=f32).astype(bf16)
            out_ref[:, pl.ds(pl.multiple_of(g * GROUP, GROUP), GROUP), :] = natural.reshape(
                channels, GROUP, cols
            )

    for layer in range(layers):
        packs[layer] = pack[...].astype(bf16)
        halos = halo_copies(layer)
        for copy in halos:
            copy.start()
        row_transform(layer)

        @pl.loop(1, devices)
        def _(k):
            a2a_copy(layer, k).start()

        for copy in halos:
            copy.wait_recv()
        carry[:, :, :LANES] = jnp.zeros((2, pair, LANES), f32)
        carry[:, :, LANES + cols :] = jnp.zeros((2, pair, LANES), f32)

        @pl.loop(0, groups)
        def _(g):
            before, after = hcol[layer, 0].astype(f32), hcol[layer, 1].astype(f32)
            heads, tails = [], []
            for p in range(2):
                k = 2 * g + p
                heads.append(pltpu.roll(before, (2 * LANES - 4 - 4 * k) % LANES, 1))
                tails.append(pltpu.roll(after, (LANES - 4 * k) % LANES, 1))
            store_rows(g, heads[0], heads[1], 0)
            store_rows(g, tails[0], tails[1], LANES + cols)

        above, below = hrow[layer, 0].astype(f32), hrow[layer, 1].astype(f32)

        def patch(ref_rows, halo):
            return jnp.concatenate([halo, ref_rows.astype(f32)[pair:]], axis=0).astype(bf16)

        nst[: 2 * pair, :] = patch(nst[: 2 * pair, :], above[pair:])
        end = groups * whole
        nst[end : end + 2 * pair, :] = jnp.concatenate([carry[1], below[:pair]], axis=0).astype(bf16)
        end = groups * half
        for p in range(2):
            side = slice(p * pair, (p + 1) * pair)
            fst[p, : 2 * pair, :] = patch(fst[p, : 2 * pair, :], above[side])
            fst[p, end : end + 2 * pair, :] = jnp.concatenate(
                [carry[p], below[side]], axis=0
            ).astype(bf16)

        cut = first_part * groups // 16

        @pl.loop(0, cut)
        def _(g):
            conv_group(layer, g)

        mix_modes(layer)

        @pl.loop(cut, groups)
        def _(g):
            conv_group(layer, g)

        inverse_rows(layer)
        carry[...] = jnp.zeros_like(carry)
        pack[...] = jnp.zeros_like(pack)

        @pl.loop(0, groups)
        def _(g):
            finish_group(layer, g)

        for copy in halos:
            copy.wait_send()

        @pl.loop(1, devices)
        def _(k):
            a2a_copy(layer, k).wait_send()
            gather_copy(layer, k).wait_send()


def main_call(u, weights, near, far, order, back, fwd, ftab, itab, inv, bias, mixture, sizes):
    channels, local_rows, cols = u.shape
    layers = weights.shape[0]
    devices = sizes[0] * sizes[1]
    pair = 2 * channels
    slot = (channels + 7) // 8 * 8
    blocks = devices * min(weights.shape[-1], MODES_Y) // MODES_Y
    groups = local_rows // GROUP
    wide = cols + 2 * LANES
    vmem = pl.BlockSpec(memory_space=pltpu.VMEM)
    smem = pl.BlockSpec(memory_space=pltpu.SMEM)
    dma = pltpu.SemaphoreType.DMA
    return pl.pallas_call(
        functools.partial(main_kernel, sizes=sizes, first_part=8),
        name="operator",
        out_shape=jax.ShapeDtypeStruct(u.shape, bf16),
        in_specs=[vmem] * 11 + [smem],
        out_specs=vmem,
        scratch_shapes=[
            pltpu.VMEM((groups * 8 * pair + 2 * pair, wide), bf16),
            pltpu.VMEM((2, groups * 4 * pair + 2 * pair, wide), bf16),
            pltpu.VMEM((groups * 8 * pair, cols), f32),
            pltpu.VMEM((groups * 8 * pair, LANES), f32),
            pltpu.VMEM((groups * 8 * pair, LANES), f32),
            pltpu.VMEM((2, pair, wide), f32),
            pltpu.VMEM((2, 4 * pair, LANES), f32),
            pltpu.VMEM((layers, 2, 4 * pair, LANES), bf16),
            pltpu.VMEM((layers, 2, 2 * pair, cols), bf16),
            pltpu.VMEM((layers, 2, 4 * pair, LANES), bf16),
            pltpu.VMEM((layers, 2, 2 * pair, wide), bf16),
            pltpu.VMEM((layers, blocks * slot, LANES), f32),
            pltpu.VMEM((layers, devices - 1, slot, LANES), f32),
            pltpu.VMEM((layers, slot, LANES), f32),
            pltpu.VMEM((layers, devices * slot, LANES), f32),
            dma((layers, 8)),
            dma((layers, 8)),
            dma((layers, devices - 1)),
            dma((layers, devices - 1)),
            dma((layers, devices - 1)),
            dma((layers, devices - 1)),
        ],
        compiler_params=pltpu.CompilerParams(
            collective_id=0, has_side_effects=True, vmem_limit_bytes=62 * 1024 * 1024
        ),
    )(u, weights, near, far, order, back, fwd, ftab, itab, inv, bias, mixture)


def solution(mesh):
    sizes = (mesh.shape["gx"], mesh.shape["gy"])

    def on_device(grid_field, spectral_weight, conv_near, conv_far, mix_logits, channel_bias):
        _, channels, local_rows, local_cols = grid_field.shape
        share = spectral_weight.shape[-1]
        devices = sizes[0] * sizes[1]
        cells_x, cells_y = local_rows * sizes[0], local_cols * sizes[1]
        modes_x = share * devices // MODES_Y
        per_share = max(share // MODES_Y, 1)
        blocks = modes_x // per_share
        groups = local_rows // GROUP
        assert share * per_share in (16, 32, 128)
        assert groups * GROUP == local_rows and 8 * groups <= LANES

        lower = jnp.arange(modes_x // 2, dtype=jnp.int32)
        row_modes = jnp.concatenate([lower, lower + (cells_x - modes_x // 2)])
        row_modes = row_modes.reshape(blocks, per_share).T.reshape(modes_x)
        col_modes = jnp.arange(MODES_Y, dtype=jnp.int32)
        index = jnp.arange(local_rows, dtype=jnp.int32)
        inner = index % GROUP
        in_group = (inner % 8) // 2 * 4 + inner % 2 * 2 + inner // 8
        row_at = lax.axis_index("gx") * local_rows + index // GROUP * GROUP + in_group
        col_at = lax.axis_index("gy") * local_cols + jnp.arange(local_cols, dtype=jnp.int32)
        row_phase = (row_modes[:, None] * row_at[None, :] % cells_x).astype(f32) * (
            full_turn / cells_x
        )
        row_table = jnp.concatenate([jnp.cos(row_phase), jnp.sin(row_phase)], axis=0)
        high, low = split_bf16(row_table)
        ftab = jnp.concatenate([high, high, low], axis=1)
        itab = jnp.concatenate([high.T, high.T, low.T], axis=1)
        col_phase = (col_at[:, None] * col_modes[None, :] % cells_y).astype(f32) * (
            full_turn / cells_y
        )
        cosine, sine = jnp.cos(col_phase), -jnp.sin(col_phase)
        fwd = jnp.concatenate([cosine, sine, sine, -cosine], axis=1).astype(bf16)
        col_weight = jnp.where(col_modes == 0, 1.0, 2.0).astype(f32) / (cells_x * cells_y)
        inverse = jnp.concatenate([cosine * col_weight, sine * col_weight], axis=1).T
        high, low = split_bf16(inverse)
        inv = jnp.concatenate([high, high, low], axis=0)

        at = jnp.arange(GROUP * channels, dtype=jnp.int32)
        inner = at // channels
        natural = at % channels * GROUP + (inner % 8) // 2 * 4 + inner % 2 * 2 + inner // 8
        order = (natural[:, None] == at[None, :]).astype(bf16)
        back = (natural[None, :] == at[:, None]).astype(bf16)

        exponents = jnp.exp(mix_logits)
        mixtures = exponents / jnp.sum(exponents, axis=1, keepdims=True)
        bias = jnp.tile(channel_bias, (1, 8))[:, :, None]
        near, far = prep_call(conv_near, conv_far)
        field = main_call(
            grid_field[0], spectral_weight, near, far, order, back, fwd, ftab, itab, inv, bias,
            mixtures, sizes,
        )
        return field[None]

    in_specs = (
        P(None, None, "gx", "gy"),
        P(None, None, None, None, ("gx", "gy")),
        P(),
        P(),
        P(),
        P(),
    )
    return jax.shard_map(
        on_device,
        mesh=mesh,
        in_specs=in_specs,
        out_specs=P(None, None, "gx", "gy"),
        check_vma=False,
    )
```

```python
import functools
import math

import jax
import jax.numpy as jnp
from jax import lax
from jax.experimental import pallas as pl
from jax.experimental.pallas import tpu as pltpu
from jax.sharding import PartitionSpec as P

full_turn = 2.0 * math.pi
MESH = pl.DeviceIdType.MESH
MODES_Y = 32
GROUP = 16
LANES = 128
HALO = 4
NEAR = (-1, 0, 1)
FAR = (-4, -2, 0, 2, 4)
f32 = jnp.float32
bf16 = jnp.bfloat16


def split_bf16(value):
    high = value.astype(bf16)
    low = (value - high.astype(f32)).astype(bf16)
    return high, low


def restore_kernel(value_ref, back_ref, columns_ref, out_ref):
    value = jnp.dot(value_ref[...], columns_ref[...], preferred_element_type=f32).astype(bf16)
    value = jnp.dot(back_ref[...], value, preferred_element_type=f32).astype(bf16)
    out_ref[...] = value.reshape(out_ref.shape)


def restore_call(value, back, columns, channels):
    whole = channels * GROUP
    groups, cols = value.shape[0] // whole, value.shape[1]
    vmem = pl.BlockSpec(memory_space=pltpu.VMEM)
    return pl.pallas_call(
        restore_kernel,
        grid=(groups,),
        name="restore",
        in_specs=[pl.BlockSpec((whole, cols), lambda i: (i, 0)), vmem, vmem],
        out_specs=pl.BlockSpec((channels, GROUP, cols), lambda i: (0, i, 0)),
        out_shape=jax.ShapeDtypeStruct((channels, groups * GROUP, cols), bf16),
    )(value, back, columns)


def main_kernel(
    u_ref, sw_ref, near_ref, far_ref, order_ref, columns_ref, stack_ref, rtab_ref, ctab_ref,
    mix_ref, bias_ref, out_ref,
    ubuf, obuf, nst, fst, conv, lhs, lines, carry, pack, packs, edges, hcol, hrow, hcorner,
    sendbuf, recv, mixed, gath, nw, fw, taps, tall, ftab, itab, fwd, inv, mixb, biasb, code, pairs,
    u_sem, out_sem, halo_send, halo_recv, a2a_send, a2a_recv, gat_send, gat_recv,
    *, sizes, cells, first_part, batch,
):
    gx, gy = sizes
    devices = gx * gy
    layers = sw_ref.shape[0]
    channels, local_rows, cols = ubuf.shape
    pair = 2 * channels
    half = 4 * pair
    whole = 2 * half
    groups = local_rows // GROUP
    planes = cols // LANES
    edge = HALO // planes
    slot = mixed.shape[1]
    blocks = sendbuf.shape[1] // slot
    sharers = devices // blocks
    per_device = 2 * MODES_Y
    modes_x = rtab_ref.shape[0] // 2
    share_rows = modes_x // blocks
    share = sw_ref.shape[-1]
    trim = (pair + 15) // 16 * 16
    my_x, my_y = lax.axis_index("gx"), lax.axis_index("gy")
    me = my_x * gy + my_y

    def place(index):
        return (index // gy, index % gy)

    barrier = pltpu.get_barrier_semaphore()

    @pl.loop(1, devices)
    def _(k):
        pl.semaphore_signal(
            barrier, inc=1, device_id=place((me + k) % devices), device_id_type=MESH
        )

    def u_copy(g):
        rows = pl.ds(pl.multiple_of(g * GROUP, GROUP), GROUP)
        return pltpu.make_async_copy(u_ref.at[:, rows, :], ubuf.at[:, rows, :], u_sem.at[g])

    @pl.loop(0, groups)
    def _(g):
        u_copy(g).start()

    def iota(shape, dim):
        return lax.broadcasted_iota(jnp.int32, shape, dim)

    high, low = split_bf16(rtab_ref[...])
    ftab[...] = jnp.concatenate([high, high, low], axis=1)
    high, low = split_bf16(rtab_ref[...].T)
    itab[...] = jnp.concatenate([high, high, low], axis=1)
    fwd[...] = ctab_ref[...].astype(bf16)
    turned_cols = ctab_ref[...].T[:per_device]
    weight = jnp.where(iota((per_device, cols), 0) % MODES_Y == 0, 1.0, 2.0) / cells
    high, low = split_bf16(turned_cols * weight)
    inv[...] = jnp.concatenate([high, high, low], axis=0)

    exponents = jnp.exp(mix_ref[...])
    mixtures = exponents / jnp.sum(exponents, axis=1, keepdims=True)
    for layer in range(layers):
        for i in range(3):
            at = 3 * layer + i
            mixb[at : at + 1, :] = jnp.broadcast_to(
                mixtures[layer : layer + 1, i : i + 1], (1, cols)
            )
        same = iota((half, channels), 0) % channels == iota((half, channels), 1)
        column = jnp.sum(
            jnp.where(same, bias_ref[layer : layer + 1, :], 0.0), axis=1, keepdims=True
        )
        biasb[layer] = jnp.broadcast_to(column, (half, LANES))

    at, lane_at = iota(code.shape, 0), iota(code.shape, 1)
    plane, lane = lane_at // LANES, lane_at % LANES
    before = planes * (lane - (LANES - edge)) + plane
    after = planes * lane + plane
    code[...] = jnp.where(
        (at < LANES) & (lane >= LANES - edge),
        at - before,
        jnp.where((at >= LANES) & (lane < edge), at - LANES - after, -1),
    )

    def edge_pick(k):
        return jnp.where(code[...] == HALO * k, 1.0, 0.0).astype(bf16)

    depth = 6 * pair
    wide = (depth + LANES - 1) // LANES * LANES

    def tap_rows(taps_ref):
        count = taps_ref.shape[2]
        for o in range(channels):
            taps[layers * o : layers * (o + 1), :count] = taps_ref[o].astype(f32)
        return taps[:, :count].astype(bf16)

    rows_of = layers * channels

    def spread(out_ref, index):
        stacked = tall[...].astype(bf16)
        full = jnp.dot(stack_ref[...], stacked, preferred_element_type=f32).astype(bf16)
        return [full[layer * half : (layer + 1) * half, :depth] for layer in range(layers)]

    def emit(out_ref, pieces):
        for layer in range(layers):
            out_ref[layer] = jnp.concatenate([piece[layer] for piece in pieces], axis=1)

    source = tap_rows(far_ref)
    count = far_ref.shape[2]
    target = iota((count, wide), 1)
    base = jnp.where(
        target < 5 * channels,
        target // channels * (5 * channels) + target % channels,
        -count,
    )
    base = iota((count, wide), 0) - base
    pieces = []
    for column in range(5):
        pick = jnp.where(base == column * channels, 1.0, 0.0).astype(bf16)
        block = jnp.dot(source, pick, preferred_element_type=f32)
        for row in range(8):
            tall[rows_of * row : rows_of * (row + 1), :] = (
                pltpu.roll(block, channels * row, 1) if row else block
            )
        pieces.append(spread(fw, column))
    emit(fw, pieces)

    source = tap_rows(near_ref)
    count = near_ref.shape[2]
    target = iota((count, wide), 1)
    spot, channel = target // channels, target % channels
    where_row = {-1: 1, 0: 2, 1: 4, 2: 3, 3: 5, 4: 6}
    bases = []
    for row in range(4):
        tap = jnp.full(target.shape, -count, jnp.int32)
        for step in range(3):
            tap = jnp.where(
                spot == where_row[row + step - 1], step * 3 * channels + channel, tap
            )
        bases.append(iota((count, wide), 0) - tap)
    pieces = []
    for column in range(3):
        for row in range(4):
            pick = jnp.where(bases[row] == column * channels, 1.0, 0.0).astype(bf16)
            block = jnp.dot(source, pick, preferred_element_type=f32)
            for quad in range(2):
                full_row = 4 * quad + row
                index = full_row % 2 * 4 + full_row // 2
                tall[rows_of * index : rows_of * (index + 1), :] = (
                    pltpu.roll(block, 4 * channels, 1) if quad else block
                )
        pieces.append(spread(nw, column))
    emit(nw, pieces)

    def near_edges(value):
        low_lanes = iota((value.shape[0], LANES), 1) < LANES // 2
        return jnp.where(low_lanes, value[:, :LANES], value[:, cols - LANES :])

    def store_rows(g, even, odd, side):
        at = slice(side * cols, (side + 1) * cols)
        old_even, old_odd = carry[0, :, at], carry[1, :, at]
        q = [(even[i * pair : (i + 1) * pair], odd[i * pair : (i + 1) * pair]) for i in range(4)]
        near_rows = [old_odd]
        for i in range(4):
            near_rows.append(q[i][0])
            if i < 3:
                near_rows.append(q[i][1])
        near_rows = jnp.concatenate(near_rows, axis=0)
        near_at = pl.ds(pl.multiple_of(g * whole, whole), whole)
        if side:
            nst[near_at, cols:] = near_edges(near_rows).astype(bf16)
        else:
            nst[near_at, :cols] = near_rows.astype(bf16)
        row = pl.ds(pl.multiple_of(g * half, half), half)
        fst[0, row, at] = jnp.concatenate([old_even, even[: 3 * pair]], axis=0).astype(bf16)
        fst[1, row, at] = jnp.concatenate([old_odd, odd[: 3 * pair]], axis=0).astype(bf16)
        carry[0, :, at] = q[3][0]
        carry[1, :, at] = q[3][1]

    def ingest(g, value, layer):
        full = value.astype(f32)
        even, odd = full[:half], full[half:]
        store_rows(g, even, odd, 0)
        lines[pl.ds(pl.multiple_of(g * whole, whole), whole), :] = jnp.dot(
            value, fwd[...], preferred_element_type=f32
        )
        total = pack[...]
        for p in range(2):
            total = total + lax.dot_general(
                value[p * half : (p + 1) * half],
                edge_pick(2 * g + p),
                (((1,), (1,)), ((), ())),
                preferred_element_type=f32,
            )
        pack[...] = total

        @pl.when(g == 0)
        def _():
            edges[layer, 0] = jnp.concatenate([even[:pair], odd[:pair]], axis=0).astype(bf16)

        @pl.when(g == groups - 1)
        def _():
            edges[layer, 1] = jnp.concatenate(
                [even[3 * pair :], odd[3 * pair :]], axis=0
            ).astype(bf16)

    carry[...] = jnp.zeros_like(carry)
    pack[...] = jnp.zeros_like(pack)

    @pl.loop(0, groups)
    def _(g):
        u_copy(g).wait()
        slab = ubuf[:, pl.ds(pl.multiple_of(g * GROUP, GROUP), GROUP), :].reshape(whole, cols)
        value = jnp.dot(order_ref[...], slab, preferred_element_type=f32).astype(bf16)
        value = jnp.dot(value, columns_ref[...], preferred_element_type=f32).astype(bf16)
        ingest(g, value, 0)

    pl.semaphore_wait(barrier, devices - 1)

    up, down = (my_x + gx - 1) % gx, (my_x + 1) % gx
    left, right = (my_y + gy - 1) % gy, (my_y + 1) % gy

    def halo_copies(layer):
        def copy(i, src, dst, target):
            return pltpu.make_async_remote_copy(
                src_ref=src, dst_ref=dst, send_sem=halo_send.at[layer, i],
                recv_sem=halo_recv.at[layer, i], device_id=target, device_id_type=MESH,
            )

        mine, beside = packs.at[layer], hcol.at[layer]
        above, below = hcorner.at[layer, 0], hcorner.at[layer, 1]
        lasts, firsts = slice(0, LANES), slice(LANES, 2 * LANES)
        head, tail = slice(0, trim), slice(half - trim, half)
        return [
            copy(0, mine.at[:, firsts], beside.at[:, firsts], (my_x, left)),
            copy(1, mine.at[:, lasts], beside.at[:, lasts], (my_x, right)),
            copy(2, edges.at[layer, 0], hrow.at[layer, 1], (up, my_y)),
            copy(3, edges.at[layer, 1], hrow.at[layer, 0], (down, my_y)),
            copy(4, mine.at[head, firsts], below.at[:, firsts], (up, left)),
            copy(5, mine.at[tail, firsts], above.at[:, firsts], (down, left)),
            copy(6, mine.at[head, lasts], below.at[:, lasts], (up, right)),
            copy(7, mine.at[tail, lasts], above.at[:, lasts], (down, right)),
        ]

    def a2a_copy(layer, k):
        target = (me + k) % devices
        return pltpu.make_async_remote_copy(
            src_ref=sendbuf.at[layer, pl.ds(target // sharers * slot, slot)],
            dst_ref=recv.at[layer, k - 1],
            send_sem=a2a_send.at[layer, k - 1],
            recv_sem=a2a_recv.at[layer, k - 1],
            device_id=place(target),
            device_id_type=MESH,
        )

    def gather_copy(layer, k):
        return pltpu.make_async_remote_copy(
            src_ref=mixed.at[layer],
            dst_ref=gath.at[layer, pl.ds(me * slot, slot)],
            send_sem=gat_send.at[layer, k - 1],
            recv_sem=gat_recv.at[layer, k - 1],
            device_id=place((me + k) % devices),
            device_id_type=MESH,
        )

    def turned(value):
        return jnp.where(
            (iota(value.shape, 1) // MODES_Y) % 2 == 1,
            pltpu.roll(value, MODES_Y, 1),
            -pltpu.roll(value, LANES - MODES_Y, 1),
        )

    def triple(value):
        high, low = split_bf16(value)
        return jnp.concatenate([high, low, high], axis=0)

    def row_transform(layer):
        @pl.loop(0, channels // batch)
        def _(b):
            parts = [
                triple(lines[pl.ds(b * batch + i, local_rows, stride=channels), :])
                for i in range(batch)
            ]
            result = jnp.dot(
                ftab[...], jnp.concatenate(parts, axis=1), preferred_element_type=f32
            )
            for i in range(batch):
                both = result[:, i * LANES : (i + 1) * LANES]
                total = both[:modes_x] + pltpu.roll(both[modes_x:], per_device, 1)
                block = total
                if share_rows == 2:
                    block = jnp.where(
                        iota((blocks, LANES), 1) < per_device,
                        total[:blocks],
                        pltpu.roll(total[blocks:], per_device, 1),
                    )
                sendbuf[layer, pl.ds(b * batch + i, blocks, stride=slot), :] = block

    def mix_modes(layer):
        own = sendbuf[layer, pl.ds(pl.multiple_of(me // sharers * slot, 8), slot), :]

        @pl.loop(1, devices)
        def _(k):
            a2a_copy(layer, k).wait_recv()

        own = own + jnp.sum(recv[layer], axis=0)
        crossed = turned(own)
        is_real = iota((2 * channels, LANES), 0) % 2 == 0

        def spread_lanes(part):
            if share_rows == 1:
                tiled = jnp.concatenate([part] * (LANES // share), axis=1)
                at = iota(tiled.shape, 1) // share
                return jnp.where(at % sharers == me % sharers, tiled, 0.0)
            pieces = []
            for j in range(share_rows):
                piece = part[:, j * MODES_Y : (j + 1) * MODES_Y]
                pieces += [piece, piece]
            return jnp.concatenate(pieces, axis=1)

        total = jnp.zeros((2 * channels, LANES), f32)
        for c in range(channels):
            weights = spread_lanes(sw_ref[layer, c].reshape(2 * channels, share))
            total = total + weights * jnp.where(is_real, own[c : c + 1], crossed[c : c + 1])
        pairs[...] = total
        total = pairs[pl.ds(0, channels, stride=2), :] + pairs[pl.ds(1, channels, stride=2), :]
        total = total * mixb[3 * layer : 3 * layer + 1, :LANES]
        mixed[layer, :channels, :] = total
        gath[layer, pl.ds(pl.multiple_of(me * slot, 8), channels), :] = total

        @pl.loop(1, devices)
        def _(k):
            gather_copy(layer, k).start()

    def inverse_rows(layer):
        @pl.loop(1, devices)
        def _(k):
            gather_copy(layer, k).wait_recv()

        @pl.loop(0, channels // batch)
        def _(b):
            parts = []
            for i in range(batch):
                o = b * batch + i
                block = gath[layer, pl.ds(o, blocks, stride=slot * sharers), :]
                for j in range(1, sharers):
                    block = block + gath[layer, pl.ds(j * slot + o, blocks, stride=slot * sharers), :]
                cross = turned(block)
                stack = [block, cross]
                if share_rows == 2:
                    stack = [block, pltpu.roll(block, per_device, 1)]
                    stack += [cross, pltpu.roll(cross, per_device, 1)]
                parts.append(triple(jnp.concatenate(stack, axis=0)))
            result = jnp.dot(
                itab[...], jnp.concatenate(parts, axis=1), preferred_element_type=f32
            )
            for i in range(batch):
                lhs[pl.ds(b * batch + i, local_rows, stride=channels), :] = result[
                    :, i * LANES : (i + 1) * LANES
                ]

    def conv_group(layer, g):
        def window(rows, shifts, beside):
            own = [rows[:, s * LANES : (s + 1) * LANES] for s in range(planes)]
            at = iota((depth, LANES), 1)
            known = {}

            def piece(s, d):
                q = s + d
                plane, move = q % planes, q // planes
                if (plane, move) not in known:
                    value = own[plane]
                    if move > 0:
                        value = jnp.where(at < move, beside(plane), value)
                    if move < 0:
                        value = jnp.where(at >= LANES + move, beside(plane), value)
                    if move:
                        value = pltpu.roll(value, (-move) % LANES, 1)
                    known[plane, move] = value
                return known[plane, move]

            return jnp.concatenate(
                [
                    jnp.concatenate([piece(s, d) for s in range(planes)], axis=1)
                    for d in shifts
                ],
                axis=0,
            )

        near = []
        for h in range(2):
            rows = nst[pl.ds(pl.multiple_of(g * whole, whole) + h * half, depth), :]
            columns = window(rows, NEAR, lambda plane: rows[:, cols:])
            near.append(jnp.dot(nw[layer], columns, preferred_element_type=f32))
        parts = []
        bias = jnp.concatenate([biasb[layer]] * planes, axis=1)
        for p in range(2):
            rows = fst[p, pl.ds(pl.multiple_of(g * half, half), depth), :]
            columns = window(
                rows, FAR, lambda s: rows[:, cols + s * LANES : cols + (s + 1) * LANES]
            )
            far = jnp.dot(fw[layer], columns, preferred_element_type=f32)
            side = slice(p * 2 * pair, (p + 1) * 2 * pair)
            close = jnp.concatenate([near[0][side], near[1][side]], axis=0)
            total = (
                mixb[3 * layer + 1 : 3 * layer + 2, :] * close
                + mixb[3 * layer + 2 : 3 * layer + 3, :] * far
                + bias
            )
            parts.append(total)
        conv[pl.ds(pl.multiple_of(g * whole, whole), whole), :] = jnp.concatenate(parts, axis=0)

    def out_copy(g):
        rows = pl.ds(pl.multiple_of(g * whole, whole), whole)
        return pltpu.make_async_copy(obuf.at[rows], out_ref.at[rows], out_sem.at[g])

    def finish_group(layer, g):
        at = pl.ds(pl.multiple_of(g * whole, whole), whole)
        high, low = split_bf16(lhs[at, :per_device])
        spectral = jnp.dot(
            jnp.concatenate([high, low, high], axis=1), inv[...], preferred_element_type=f32
        )
        value = conv[at, :] + spectral
        value = (value * 0.5 * (1.0 + lax.erf(value * (0.5**0.5)))).astype(bf16)
        if layer + 1 < layers:
            ingest(g, value, layer + 1)
        else:
            obuf[at, :] = value
            out_copy(g).start()

    for layer in range(layers):
        packs[layer] = pack[...].astype(bf16)
        halos = halo_copies(layer)
        for copy in halos:
            copy.start()
        row_transform(layer)

        @pl.loop(1, devices)
        def _(k):
            a2a_copy(layer, k).start()

        for copy in halos:
            copy.wait_recv()
        carry[:, :, cols:] = jnp.zeros((2, pair, cols), f32)

        @pl.loop(0, groups)
        def _(g):
            beside = hcol[layer]
            parts = [
                jnp.dot(beside, edge_pick(2 * g + p), preferred_element_type=f32)
                for p in range(2)
            ]
            store_rows(g, parts[0], parts[1], 1)

        def halo_rows(side):
            k = 0 if side else 2 * (groups - 1)
            main = hrow[layer, side].astype(f32)
            out = []
            for p in range(2):
                corner = jnp.dot(
                    hcorner[layer, side], edge_pick(k + p), preferred_element_type=f32
                )
                corner = corner[:pair] if side else corner[trim - pair :]
                out.append((main[p * pair : (p + 1) * pair], corner))
            return out

        above, below = halo_rows(0), halo_rows(1)
        first = slice(0, 2 * pair)

        def patch(rows, halo):
            return jnp.concatenate([halo, rows.astype(f32)[pair:]], axis=0).astype(bf16)

        nst[first, :cols] = patch(nst[first, :cols], above[1][0])
        nst[first, cols:] = patch(nst[first, cols:], near_edges(above[1][1]))
        end = groups * whole
        last = slice(end, end + 2 * pair)
        nst[last, :cols] = jnp.concatenate([carry[1, :, :cols], below[0][0]], axis=0).astype(bf16)
        nst[last, cols:] = near_edges(
            jnp.concatenate([carry[1, :, cols:], below[0][1]], axis=0)
        ).astype(bf16)
        end = groups * half
        last = slice(end, end + 2 * pair)
        for p in range(2):
            for side in range(2):
                at = slice(side * cols, (side + 1) * cols)
                fst[p, first, at] = patch(fst[p, first, at], above[p][side])
                fst[p, last, at] = jnp.concatenate(
                    [carry[p, :, at], below[p][side]], axis=0
                ).astype(bf16)

        cut = first_part * groups // 16

        @pl.loop(0, cut)
        def _(g):
            conv_group(layer, g)

        mix_modes(layer)

        @pl.loop(cut, groups)
        def _(g):
            conv_group(layer, g)

        inverse_rows(layer)
        carry[...] = jnp.zeros_like(carry)
        pack[...] = jnp.zeros_like(pack)

        @pl.loop(0, groups)
        def _(g):
            finish_group(layer, g)

        for copy in halos:
            copy.wait_send()

        @pl.loop(1, devices)
        def _(k):
            a2a_copy(layer, k).wait_send()
            gather_copy(layer, k).wait_send()

    @pl.loop(0, groups)
    def _(g):
        out_copy(g).wait()


def main_call(u, weights, near, far, order, columns, stack, rtab, ctab, mix, bias, sizes, cells):
    channels, local_rows, cols = u.shape
    layers = weights.shape[0]
    devices = sizes[0] * sizes[1]
    pair = 2 * channels
    half = 4 * pair
    slot = (channels + 7) // 8 * 8
    blocks = devices * min(weights.shape[-1], MODES_Y) // MODES_Y
    groups = local_rows // GROUP
    modes_x = rtab.shape[0] // 2
    depth = 6 * pair
    wide = (depth + LANES - 1) // LANES * LANES
    trim = (pair + 15) // 16 * 16
    vmem = pl.BlockSpec(memory_space=pltpu.VMEM)
    anywhere = pl.BlockSpec(memory_space=pl.ANY)
    dma = pltpu.SemaphoreType.DMA
    scratch = pltpu.VMEM
    return pl.pallas_call(
        functools.partial(
            main_kernel, sizes=sizes, cells=cells, first_part=8,
            batch=4 if channels % 4 == 0 else 1,
        ),
        name="operator",
        out_shape=jax.ShapeDtypeStruct((groups * 2 * half, cols), bf16),
        in_specs=[anywhere] + [vmem] * 10,
        out_specs=anywhere,
        scratch_shapes=[
            scratch((channels, local_rows, cols), bf16),
            scratch((groups * 2 * half, cols), bf16),
            scratch((groups * 2 * half + 2 * pair, cols + LANES), bf16),
            scratch((2, groups * half + 2 * pair, 2 * cols), bf16),
            scratch((groups * 2 * half, cols), f32),
            scratch((groups * 2 * half, LANES), f32),
            scratch((groups * 2 * half, LANES), f32),
            scratch((2, pair, 2 * cols), f32),
            scratch((half, 2 * LANES), f32),
            scratch((layers, half, 2 * LANES), bf16),
            scratch((layers, 2, 2 * pair, cols), bf16),
            scratch((layers, half, 2 * LANES), bf16),
            scratch((layers, 2, 2 * pair, cols), bf16),
            scratch((layers, 2, trim, 2 * LANES), bf16),
            scratch((layers, blocks * slot, LANES), f32),
            scratch((layers, devices - 1, slot, LANES), f32),
            scratch((layers, slot, LANES), f32),
            scratch((layers, devices * slot, LANES), f32),
            scratch((layers, half, 3 * depth), bf16),
            scratch((layers, half, 5 * depth), bf16),
            scratch((layers * channels, 4 * LANES), f32),
            scratch((8 * layers * channels, wide), f32),
            scratch((2 * modes_x, 3 * local_rows), bf16),
            scratch((local_rows, 6 * modes_x), bf16),
            scratch((cols, LANES), bf16),
            scratch((6 * MODES_Y, cols), bf16),
            scratch((8, cols), f32),
            scratch((layers, half, LANES), f32),
            scratch((2 * LANES, cols), jnp.int32),
            scratch((2 * channels, LANES), f32),
            dma((groups,)),
            dma((groups,)),
            dma((layers, 8)),
            dma((layers, 8)),
            dma((layers, devices - 1)),
            dma((layers, devices - 1)),
            dma((layers, devices - 1)),
            dma((layers, devices - 1)),
        ],
        compiler_params=pltpu.CompilerParams(
            collective_id=0, has_side_effects=True, vmem_limit_bytes=62 * 1024 * 1024
        ),
    )(u, weights, near, far, order, columns, stack, rtab, ctab, mix, bias)


def solution(mesh):
    sizes = (mesh.shape["gx"], mesh.shape["gy"])

    def on_device(grid_field, spectral_weight, conv_near, conv_far, mix_logits, channel_bias):
        _, channels, local_rows, local_cols = grid_field.shape
        layers = spectral_weight.shape[0]
        share = spectral_weight.shape[-1]
        devices = sizes[0] * sizes[1]
        cells_x, cells_y = local_rows * sizes[0], local_cols * sizes[1]
        modes_x = share * devices // MODES_Y
        per_share = max(share // MODES_Y, 1)
        blocks = modes_x // per_share
        groups = local_rows // GROUP
        planes = local_cols // LANES
        assert share * per_share in (16, 32, 128)
        assert groups * GROUP == local_rows and 8 * groups <= LANES
        assert planes * LANES == local_cols and planes in (1, 2, 4)

        def group_order(inner):
            return inner % 8 // 2 * 4 + inner % 2 * 2 + inner // 8

        mode = jnp.arange(2 * modes_x, dtype=jnp.int32)
        slot = mode % modes_x % blocks * per_share + mode % modes_x // blocks
        row_mode = jnp.where(slot < modes_x // 2, slot, slot + (cells_x - modes_x))
        index = jnp.arange(local_rows, dtype=jnp.int32)
        row_at = index // GROUP * GROUP + group_order(index % GROUP)
        row_at = row_at + lax.axis_index("gx") * local_rows
        phase = (row_mode[:, None] * row_at[None, :] % cells_x).astype(f32) * (full_turn / cells_x)
        rtab = jnp.where(mode[:, None] < modes_x, jnp.cos(phase), jnp.sin(phase))

        index = jnp.arange(local_cols, dtype=jnp.int32)
        spot = index % LANES * planes + index // LANES
        col_at = lax.axis_index("gy") * local_cols + spot
        lane = jnp.arange(LANES, dtype=jnp.int32)[None, :]
        phase = (col_at[:, None] * (lane % MODES_Y) % cells_y).astype(f32) * (full_turn / cells_y)
        cosine, sine = jnp.cos(phase), jnp.sin(phase)
        kind = lane // MODES_Y
        ctab = jnp.where(kind == 0, cosine, jnp.where(kind == 3, -cosine, -sine))

        at = jnp.arange(GROUP * channels, dtype=jnp.int32)
        natural = at % channels * GROUP + group_order(at // channels)
        order = (natural[:, None] == at[None, :]).astype(bf16)
        back = (natural[None, :] == at[:, None]).astype(bf16)
        columns = (index[:, None] == spot[None, :]).astype(bf16)
        columns_back = (index[None, :] == spot[:, None]).astype(bf16)
        count = 8 * channels
        at = jnp.arange(layers * count, dtype=jnp.int32)
        wanted = at % count // channels * (layers * channels)
        wanted = wanted + at % channels * layers + at // count
        stack = (wanted[:, None] == at[None, :]).astype(bf16)

        field = main_call(
            grid_field[0],
            spectral_weight.transpose(0, 2, 3, 1, 4),
            conv_near.transpose(1, 0, 2),
            conv_far.transpose(1, 0, 2),
            order, columns, stack, rtab, ctab, mix_logits, channel_bias,
            sizes, cells_x * cells_y,
        )
        return restore_call(field, back, columns_back, channels)[None]

    in_specs = (
        P(None, None, "gx", "gy"),
        P(None, None, None, None, ("gx", "gy")),
        P(),
        P(),
        P(),
        P(),
    )
    return jax.shard_map(
        on_device,
        mesh=mesh,
        in_specs=in_specs,
        out_specs=P(None, None, "gx", "gy"),
        check_vma=False,
    )
```

```python
import functools
import math

import jax
import jax.numpy as jnp
from jax import lax
from jax.experimental import pallas as pl
from jax.experimental.pallas import tpu as pltpu
from jax.sharding import PartitionSpec as P

full_turn = 2.0 * math.pi
MESH = pl.DeviceIdType.MESH
MODES_Y = 32
GROUP = 16
LANES = 128
HALO = 4
CHUNK = 4
NEAR = (-1, 0, 1)
FAR = (-4, -2, 0, 2, 4)
f32 = jnp.float32
bf16 = jnp.bfloat16


def split_bf16(value):
    high = value.astype(bf16)
    low = (value - high.astype(f32)).astype(bf16)
    return high, low


def group_order(place):
    return place % 8 // 2 * 4 + place % 2 * 2 + place // 8


def iota(shape, dim):
    return lax.broadcasted_iota(jnp.int32, shape, dim)


def natural_order(at, channels):
    return at % channels * GROUP + group_order(at // channels)


def natural_column(at, cols):
    return at % LANES * (cols // LANES) + at // LANES


def matches(left, right):
    return jnp.where(left == right, 1.0, 0.0).astype(bf16)


def restore_kernel(value_ref, out_ref, back, columns, *, chunk):
    channels, _, cols = out_ref.shape
    whole = channels * GROUP

    @pl.when(pl.program_id(0) == 0)
    def _():
        at = natural_order(iota((8, whole), 1), channels)[:1]
        back[...] = matches(iota((whole, whole), 0), at)
        at = natural_column(iota((cols, LANES), 0), cols)[:, :1]
        columns[...] = matches(at, iota((cols, cols), 1))

    for i in range(chunk):
        value = value_ref[i * whole : (i + 1) * whole, :]
        value = jnp.dot(value, columns[...], preferred_element_type=f32).astype(bf16)
        value = jnp.dot(back[...], value, preferred_element_type=f32).astype(bf16)
        out_ref[:, i * GROUP : (i + 1) * GROUP, :] = value.reshape(channels, GROUP, cols)


def restore_call(value, channels):
    whole = channels * GROUP
    groups, cols = value.shape[0] // whole, value.shape[1]
    chunk = CHUNK if groups % CHUNK == 0 else 1
    return pl.pallas_call(
        functools.partial(restore_kernel, chunk=chunk),
        grid=(groups // chunk,),
        name="restore",
        in_specs=[pl.BlockSpec((chunk * whole, cols), lambda i: (i, 0))],
        out_specs=pl.BlockSpec((channels, chunk * GROUP, cols), lambda i: (0, i, 0)),
        out_shape=jax.ShapeDtypeStruct((channels, groups * GROUP, cols), bf16),
        scratch_shapes=[pltpu.VMEM((whole, whole), bf16), pltpu.VMEM((cols, cols), bf16)],
    )(value)


def main_kernel(
    u_ref, sw_ref, near_ref, far_ref, rtab_ref, ctab_ref,
    mix_ref, bias_ref, out_ref,
    ubuf, obuf, nst, fst, conv, lhs, lines, carry, pack, packs, edges, hcol, hrow, hcorner,
    sendbuf, recv, mixed, gath, nw, fw, taps, tall, ftab, itab, fwd, inv, mixb, biasb, code, pairs,
    order, columns, stack,
    u_sem, out_sem, halo_send, halo_recv, a2a_send, a2a_recv, gat_send, gat_recv,
    *, sizes, cells, first_part, batch,
):
    gx, gy = sizes
    devices = gx * gy
    layers = sw_ref.shape[0]
    channels, local_rows, cols = ubuf.shape
    pair = 2 * channels
    half = 4 * pair
    whole = 2 * half
    groups = local_rows // GROUP
    planes = cols // LANES
    edge = HALO // planes
    slot = mixed.shape[1]
    blocks = sendbuf.shape[1] // slot
    sharers = devices // blocks
    per_device = 2 * MODES_Y
    modes_x = rtab_ref.shape[0] // 2
    share_rows = modes_x // blocks
    share = sw_ref.shape[-1]
    trim = (pair + 15) // 16 * 16
    my_x, my_y = lax.axis_index("gx"), lax.axis_index("gy")
    me = my_x * gy + my_y

    def place(index):
        return (index // gy, index % gy)

    barrier = pltpu.get_barrier_semaphore()

    @pl.loop(1, devices)
    def _(k):
        pl.semaphore_signal(
            barrier, inc=1, device_id=place((me + k) % devices), device_id_type=MESH
        )

    def u_copy(g):
        rows = pl.ds(pl.multiple_of(g * GROUP, GROUP), GROUP)
        return pltpu.make_async_copy(u_ref.at[:, rows, :], ubuf.at[:, rows, :], u_sem.at[g])

    @pl.loop(0, groups)
    def _(g):
        u_copy(g).start()

    at = natural_order(iota((whole, LANES), 0), channels)[:, :1]
    order[...] = matches(at, iota((whole, whole), 1))
    at = natural_column(iota((8, cols), 1), cols)[:1]
    columns[...] = matches(iota((cols, cols), 0), at)
    at = iota((layers * half, LANES), 0)
    wanted = at % half // channels * (layers * channels) + at % channels * layers + at // half
    stack[...] = matches(wanted[:, :1], iota(stack.shape, 1))

    high, low = split_bf16(rtab_ref[...])
    ftab[...] = jnp.concatenate([high, high, low], axis=1)
    high, low = split_bf16(rtab_ref[...].T)
    itab[...] = jnp.concatenate([high, high, low], axis=1)
    fwd[...] = ctab_ref[...].astype(bf16)
    turned_cols = ctab_ref[...].T[:per_device]
    weight = jnp.where(iota((per_device, cols), 0) % MODES_Y == 0, 1.0, 2.0) / cells
    high, low = split_bf16(turned_cols * weight)
    inv[...] = jnp.concatenate([high, high, low], axis=0)

    exponents = jnp.exp(mix_ref[...])
    mixtures = exponents / jnp.sum(exponents, axis=1, keepdims=True)
    for layer in range(layers):
        for i in range(3):
            at = 3 * layer + i
            mixb[at : at + 1, :] = jnp.broadcast_to(
                mixtures[layer : layer + 1, i : i + 1], (1, cols)
            )
        same = iota((half, channels), 0) % channels == iota((half, channels), 1)
        column = jnp.sum(
            jnp.where(same, bias_ref[layer : layer + 1, :], 0.0), axis=1, keepdims=True
        )
        biasb[layer] = jnp.broadcast_to(column, (half, LANES))

    at, lane_at = iota(code.shape, 0), iota(code.shape, 1)
    plane, lane = lane_at // LANES, lane_at % LANES
    before = planes * (lane - (LANES - edge)) + plane
    after = planes * lane + plane
    code[...] = jnp.where(
        (at < LANES) & (lane >= LANES - edge),
        at - before,
        jnp.where((at >= LANES) & (lane < edge), at - LANES - after, -1),
    )

    def edge_pick(k):
        return jnp.where(code[...] == HALO * k, 1.0, 0.0).astype(bf16)

    depth = 6 * pair
    wide = (depth + LANES - 1) // LANES * LANES

    def tap_rows(taps_ref):
        count = taps_ref.shape[2]
        for o in range(channels):
            taps[layers * o : layers * (o + 1), :count] = taps_ref[o].astype(f32)
        return taps[:, :count].astype(bf16)

    rows_of = layers * channels

    def spread(out_ref, index):
        stacked = tall[...].astype(bf16)
        full = jnp.dot(stack[...], stacked, preferred_element_type=f32).astype(bf16)
        return [full[layer * half : (layer + 1) * half, :depth] for layer in range(layers)]

    def emit(out_ref, pieces):
        for layer in range(layers):
            out_ref[layer] = jnp.concatenate([piece[layer] for piece in pieces], axis=1)

    source = tap_rows(far_ref)
    count = far_ref.shape[2]
    target = iota((count, wide), 1)
    base = jnp.where(
        target < 5 * channels,
        target // channels * (5 * channels) + target % channels,
        -count,
    )
    base = iota((count, wide), 0) - base
    pieces = []
    for column in range(5):
        pick = jnp.where(base == column * channels, 1.0, 0.0).astype(bf16)
        block = jnp.dot(source, pick, preferred_element_type=f32)
        for row in range(8):
            tall[rows_of * row : rows_of * (row + 1), :] = (
                pltpu.roll(block, channels * row, 1) if row else block
            )
        pieces.append(spread(fw, column))
    emit(fw, pieces)

    source = tap_rows(near_ref)
    count = near_ref.shape[2]
    target = iota((count, wide), 1)
    spot, channel = target // channels, target % channels
    where_row = {-1: 1, 0: 2, 1: 4, 2: 3, 3: 5, 4: 6}
    bases = []
    for row in range(4):
        tap = jnp.full(target.shape, -count, jnp.int32)
        for step in range(3):
            tap = jnp.where(
                spot == where_row[row + step - 1], step * 3 * channels + channel, tap
            )
        bases.append(iota((count, wide), 0) - tap)
    pieces = []
    for column in range(3):
        for row in range(4):
            pick = jnp.where(bases[row] == column * channels, 1.0, 0.0).astype(bf16)
            block = jnp.dot(source, pick, preferred_element_type=f32)
            for quad in range(2):
                full_row = 4 * quad + row
                index = full_row % 2 * 4 + full_row // 2
                tall[rows_of * index : rows_of * (index + 1), :] = (
                    pltpu.roll(block, 4 * channels, 1) if quad else block
                )
        pieces.append(spread(nw, column))
    emit(nw, pieces)

    def near_edges(value):
        low_lanes = iota((value.shape[0], LANES), 1) < LANES // 2
        return jnp.where(low_lanes, value[:, :LANES], value[:, cols - LANES :])

    def store_rows(g, even, odd, side):
        at = slice(side * cols, (side + 1) * cols)
        old_even, old_odd = carry[0, :, at], carry[1, :, at]
        q = [(even[i * pair : (i + 1) * pair], odd[i * pair : (i + 1) * pair]) for i in range(4)]
        near_rows = [old_odd]
        for i in range(4):
            near_rows.append(q[i][0])
            if i < 3:
                near_rows.append(q[i][1])
        near_rows = jnp.concatenate(near_rows, axis=0)
        near_at = pl.ds(pl.multiple_of(g * whole, whole), whole)
        if side:
            nst[near_at, cols:] = near_edges(near_rows).astype(bf16)
        else:
            nst[near_at, :cols] = near_rows.astype(bf16)
        row = pl.ds(pl.multiple_of(g * half, half), half)
        fst[0, row, at] = jnp.concatenate([old_even, even[: 3 * pair]], axis=0).astype(bf16)
        fst[1, row, at] = jnp.concatenate([old_odd, odd[: 3 * pair]], axis=0).astype(bf16)
        carry[0, :, at] = q[3][0]
        carry[1, :, at] = q[3][1]

    def ingest(g, value, layer):
        full = value.astype(f32)
        even, odd = full[:half], full[half:]
        store_rows(g, even, odd, 0)
        lines[pl.ds(pl.multiple_of(g * whole, whole), whole), :] = jnp.dot(
            value, fwd[...], preferred_element_type=f32
        )
        total = pack[...]
        for p in range(2):
            total = total + lax.dot_general(
                value[p * half : (p + 1) * half],
                edge_pick(2 * g + p),
                (((1,), (1,)), ((), ())),
                preferred_element_type=f32,
            )
        pack[...] = total

        @pl.when(g == 0)
        def _():
            edges[layer, 0] = jnp.concatenate([even[:pair], odd[:pair]], axis=0).astype(bf16)

        @pl.when(g == groups - 1)
        def _():
            edges[layer, 1] = jnp.concatenate(
                [even[3 * pair :], odd[3 * pair :]], axis=0
            ).astype(bf16)

    carry[...] = jnp.zeros_like(carry)
    pack[...] = jnp.zeros_like(pack)

    @pl.loop(0, groups, unroll=2)
    def _(g):
        u_copy(g).wait()
        slab = ubuf[:, pl.ds(pl.multiple_of(g * GROUP, GROUP), GROUP), :].reshape(whole, cols)
        value = jnp.dot(order[...], slab, preferred_element_type=f32).astype(bf16)
        value = jnp.dot(value, columns[...], preferred_element_type=f32).astype(bf16)
        ingest(g, value, 0)

    pl.semaphore_wait(barrier, devices - 1)

    up, down = (my_x + gx - 1) % gx, (my_x + 1) % gx
    left, right = (my_y + gy - 1) % gy, (my_y + 1) % gy

    def halo_copies(layer):
        def copy(i, src, dst, target):
            return pltpu.make_async_remote_copy(
                src_ref=src, dst_ref=dst, send_sem=halo_send.at[layer, i],
                recv_sem=halo_recv.at[layer, i], device_id=target, device_id_type=MESH,
            )

        mine, beside = packs.at[layer], hcol.at[layer]
        above, below = hcorner.at[layer, 0], hcorner.at[layer, 1]
        lasts, firsts = slice(0, LANES), slice(LANES, 2 * LANES)
        head, tail = slice(0, trim), slice(half - trim, half)
        return [
            copy(0, mine.at[:, firsts], beside.at[:, firsts], (my_x, left)),
            copy(1, mine.at[:, lasts], beside.at[:, lasts], (my_x, right)),
            copy(2, edges.at[layer, 0], hrow.at[layer, 1], (up, my_y)),
            copy(3, edges.at[layer, 1], hrow.at[layer, 0], (down, my_y)),
            copy(4, mine.at[head, firsts], below.at[:, firsts], (up, left)),
            copy(5, mine.at[tail, firsts], above.at[:, firsts], (down, left)),
            copy(6, mine.at[head, lasts], below.at[:, lasts], (up, right)),
            copy(7, mine.at[tail, lasts], above.at[:, lasts], (down, right)),
        ]

    def a2a_copy(layer, k):
        target = (me + k) % devices
        return pltpu.make_async_remote_copy(
            src_ref=sendbuf.at[layer, pl.ds(target // sharers * slot, slot)],
            dst_ref=recv.at[layer, k - 1],
            send_sem=a2a_send.at[layer, k - 1],
            recv_sem=a2a_recv.at[layer, k - 1],
            device_id=place(target),
            device_id_type=MESH,
        )

    def gather_copy(layer, k):
        return pltpu.make_async_remote_copy(
            src_ref=mixed.at[layer],
            dst_ref=gath.at[layer, pl.ds(me * slot, slot)],
            send_sem=gat_send.at[layer, k - 1],
            recv_sem=gat_recv.at[layer, k - 1],
            device_id=place((me + k) % devices),
            device_id_type=MESH,
        )

    def turned(value):
        return jnp.where(
            (iota(value.shape, 1) // MODES_Y) % 2 == 1,
            pltpu.roll(value, MODES_Y, 1),
            -pltpu.roll(value, LANES - MODES_Y, 1),
        )

    def triple(value):
        high, low = split_bf16(value)
        return jnp.concatenate([high, low, high], axis=0)

    def row_transform(layer):
        @pl.loop(0, channels // batch)
        def _(b):
            parts = [
                triple(lines[pl.ds(b * batch + i, local_rows, stride=channels), :])
                for i in range(batch)
            ]
            result = jnp.dot(
                ftab[...], jnp.concatenate(parts, axis=1), preferred_element_type=f32
            )
            for i in range(batch):
                both = result[:, i * LANES : (i + 1) * LANES]
                total = both[:modes_x] + pltpu.roll(both[modes_x:], per_device, 1)
                block = total
                if share_rows == 2:
                    block = jnp.where(
                        iota((blocks, LANES), 1) < per_device,
                        total[:blocks],
                        pltpu.roll(total[blocks:], per_device, 1),
                    )
                sendbuf[layer, pl.ds(b * batch + i, blocks, stride=slot), :] = block

    def mix_modes(layer):
        own = sendbuf[layer, pl.ds(pl.multiple_of(me // sharers * slot, 8), slot), :]

        @pl.loop(1, devices)
        def _(k):
            a2a_copy(layer, k).wait_recv()

        own = own + jnp.sum(recv[layer], axis=0)
        crossed = turned(own)
        is_real = iota((2 * channels, LANES), 0) % 2 == 0

        def spread_lanes(part):
            if share_rows == 1:
                tiled = jnp.concatenate([part] * (LANES // share), axis=1)
                at = iota(tiled.shape, 1) // share
                return jnp.where(at % sharers == me % sharers, tiled, 0.0)
            pieces = []
            for j in range(share_rows):
                piece = part[:, j * MODES_Y : (j + 1) * MODES_Y]
                pieces += [piece, piece]
            return jnp.concatenate(pieces, axis=1)

        total = jnp.zeros((2 * channels, LANES), f32)
        for c in range(channels):
            weights = spread_lanes(sw_ref[layer, c].reshape(2 * channels, share))
            total = total + weights * jnp.where(is_real, own[c : c + 1], crossed[c : c + 1])
        pairs[...] = total
        total = pairs[pl.ds(0, channels, stride=2), :] + pairs[pl.ds(1, channels, stride=2), :]
        total = total * mixb[3 * layer : 3 * layer + 1, :LANES]
        mixed[layer, :channels, :] = total
        gath[layer, pl.ds(pl.multiple_of(me * slot, 8), channels), :] = total

        @pl.loop(1, devices)
        def _(k):
            gather_copy(layer, k).start()

    def inverse_rows(layer):
        @pl.loop(1, devices)
        def _(k):
            gather_copy(layer, k).wait_recv()

        @pl.loop(0, channels // batch)
        def _(b):
            parts = []
            for i in range(batch):
                o = b * batch + i
                block = gath[layer, pl.ds(o, blocks, stride=slot * sharers), :]
                for j in range(1, sharers):
                    block = block + gath[layer, pl.ds(j * slot + o, blocks, stride=slot * sharers), :]
                cross = turned(block)
                stack = [block, cross]
                if share_rows == 2:
                    stack = [block, pltpu.roll(block, per_device, 1)]
                    stack += [cross, pltpu.roll(cross, per_device, 1)]
                parts.append(triple(jnp.concatenate(stack, axis=0)))
            result = jnp.dot(
                itab[...], jnp.concatenate(parts, axis=1), preferred_element_type=f32
            )
            for i in range(batch):
                lhs[pl.ds(b * batch + i, local_rows, stride=channels), :] = result[
                    :, i * LANES : (i + 1) * LANES
                ]

    def conv_group(layer, g):
        def window(rows, shifts, beside):
            own = [rows[:, s * LANES : (s + 1) * LANES] for s in range(planes)]
            at = iota((depth, LANES), 1)
            known = {}

            def piece(s, d):
                q = s + d
                plane, move = q % planes, q // planes
                if (plane, move) not in known:
                    value = own[plane]
                    if move > 0:
                        value = jnp.where(at < move, beside(plane), value)
                    if move < 0:
                        value = jnp.where(at >= LANES + move, beside(plane), value)
                    if move:
                        value = pltpu.roll(value, (-move) % LANES, 1)
                    known[plane, move] = value
                return known[plane, move]

            return jnp.concatenate(
                [
                    jnp.concatenate([piece(s, d) for s in range(planes)], axis=1)
                    for d in shifts
                ],
                axis=0,
            )

        near = []
        for h in range(2):
            rows = nst[pl.ds(pl.multiple_of(g * whole, whole) + h * half, depth), :]
            columns = window(rows, NEAR, lambda plane: rows[:, cols:])
            near.append(jnp.dot(nw[layer], columns, preferred_element_type=f32))
        parts = []
        bias = jnp.concatenate([biasb[layer]] * planes, axis=1)
        for p in range(2):
            rows = fst[p, pl.ds(pl.multiple_of(g * half, half), depth), :]
            columns = window(
                rows, FAR, lambda s: rows[:, cols + s * LANES : cols + (s + 1) * LANES]
            )
            far = jnp.dot(fw[layer], columns, preferred_element_type=f32)
            side = slice(p * 2 * pair, (p + 1) * 2 * pair)
            close = jnp.concatenate([near[0][side], near[1][side]], axis=0)
            total = (
                mixb[3 * layer + 1 : 3 * layer + 2, :] * close
                + mixb[3 * layer + 2 : 3 * layer + 3, :] * far
                + bias
            )
            parts.append(total)
        conv[pl.ds(pl.multiple_of(g * whole, whole), whole), :] = jnp.concatenate(parts, axis=0)

    def out_copy(g):
        rows = pl.ds(pl.multiple_of(g * whole, whole), whole)
        return pltpu.make_async_copy(obuf.at[rows], out_ref.at[rows], out_sem.at[g])

    def finish_group(layer, g):
        at = pl.ds(pl.multiple_of(g * whole, whole), whole)
        high, low = split_bf16(lhs[at, :per_device])
        spectral = jnp.dot(
            jnp.concatenate([high, low, high], axis=1), inv[...], preferred_element_type=f32
        )
        value = conv[at, :] + spectral
        value = (value * 0.5 * (1.0 + lax.erf(value * (0.5**0.5)))).astype(bf16)
        if layer + 1 < layers:
            ingest(g, value, layer + 1)
        else:
            obuf[at, :] = value
            out_copy(g).start()

    for layer in range(layers):
        packs[layer] = pack[...].astype(bf16)
        halos = halo_copies(layer)
        for copy in halos:
            copy.start()
        row_transform(layer)

        @pl.loop(1, devices)
        def _(k):
            a2a_copy(layer, k).start()

        for copy in halos[:2]:
            copy.wait_recv()
        carry[:, :, cols:] = jnp.zeros((2, pair, cols), f32)

        @pl.loop(0, groups, unroll=2)
        def _(g):
            beside = hcol[layer]
            parts = [
                jnp.dot(beside, edge_pick(2 * g + p), preferred_element_type=f32)
                for p in range(2)
            ]
            store_rows(g, parts[0], parts[1], 1)

        cut = 1 + first_part * (groups - 2) // 14

        @pl.loop(1, cut)
        def _(g):
            conv_group(layer, g)

        mix_modes(layer)

        @pl.loop(cut, groups - 1)
        def _(g):
            conv_group(layer, g)

        for copy in halos[2:]:
            copy.wait_recv()

        def halo_rows(side):
            k = 0 if side else 2 * (groups - 1)
            main = hrow[layer, side].astype(f32)
            out = []
            for p in range(2):
                corner = jnp.dot(
                    hcorner[layer, side], edge_pick(k + p), preferred_element_type=f32
                )
                corner = corner[:pair] if side else corner[trim - pair :]
                out.append((main[p * pair : (p + 1) * pair], corner))
            return out

        above, below = halo_rows(0), halo_rows(1)
        first = slice(0, 2 * pair)

        def patch(rows, halo):
            return jnp.concatenate([halo, rows.astype(f32)[pair:]], axis=0).astype(bf16)

        nst[first, :cols] = patch(nst[first, :cols], above[1][0])
        nst[first, cols:] = patch(nst[first, cols:], near_edges(above[1][1]))
        end = groups * whole
        last = slice(end, end + 2 * pair)
        nst[last, :cols] = jnp.concatenate([carry[1, :, :cols], below[0][0]], axis=0).astype(bf16)
        nst[last, cols:] = near_edges(
            jnp.concatenate([carry[1, :, cols:], below[0][1]], axis=0)
        ).astype(bf16)
        end = groups * half
        last = slice(end, end + 2 * pair)
        for p in range(2):
            for side in range(2):
                at = slice(side * cols, (side + 1) * cols)
                fst[p, first, at] = patch(fst[p, first, at], above[p][side])
                fst[p, last, at] = jnp.concatenate(
                    [carry[p, :, at], below[p][side]], axis=0
                ).astype(bf16)

        @pl.loop(0, 2)
        def _(i):
            conv_group(layer, i * (groups - 1))

        inverse_rows(layer)
        carry[...] = jnp.zeros_like(carry)
        pack[...] = jnp.zeros_like(pack)

        @pl.loop(0, groups, unroll=2)
        def _(g):
            finish_group(layer, g)

        for copy in halos:
            copy.wait_send()

        @pl.loop(1, devices)
        def _(k):
            a2a_copy(layer, k).wait_send()
            gather_copy(layer, k).wait_send()

    @pl.loop(0, groups)
    def _(g):
        out_copy(g).wait()


def main_call(u, weights, near, far, rtab, ctab, mix, bias, sizes, cells):
    channels, local_rows, cols = u.shape
    layers = weights.shape[0]
    devices = sizes[0] * sizes[1]
    pair = 2 * channels
    half = 4 * pair
    slot = (channels + 7) // 8 * 8
    blocks = devices * min(weights.shape[-1], MODES_Y) // MODES_Y
    groups = local_rows // GROUP
    modes_x = rtab.shape[0] // 2
    depth = 6 * pair
    wide = (depth + LANES - 1) // LANES * LANES
    trim = (pair + 15) // 16 * 16
    vmem = pl.BlockSpec(memory_space=pltpu.VMEM)
    anywhere = pl.BlockSpec(memory_space=pl.ANY)
    dma = pltpu.SemaphoreType.DMA
    scratch = pltpu.VMEM
    return pl.pallas_call(
        functools.partial(
            main_kernel, sizes=sizes, cells=cells, first_part=5,
            batch=4 if channels % 4 == 0 else 1,
        ),
        name="operator",
        out_shape=jax.ShapeDtypeStruct((groups * 2 * half, cols), bf16),
        in_specs=[anywhere] + [vmem] * 7,
        out_specs=anywhere,
        scratch_shapes=[
            scratch((channels, local_rows, cols), bf16),
            scratch((groups * 2 * half, cols), bf16),
            scratch((groups * 2 * half + 2 * pair, cols + LANES), bf16),
            scratch((2, groups * half + 2 * pair, 2 * cols), bf16),
            scratch((groups * 2 * half, cols), f32),
            scratch((groups * 2 * half, LANES), f32),
            scratch((groups * 2 * half, LANES), f32),
            scratch((2, pair, 2 * cols), f32),
            scratch((half, 2 * LANES), f32),
            scratch((layers, half, 2 * LANES), bf16),
            scratch((layers, 2, 2 * pair, cols), bf16),
            scratch((layers, half, 2 * LANES), bf16),
            scratch((layers, 2, 2 * pair, cols), bf16),
            scratch((layers, 2, trim, 2 * LANES), bf16),
            scratch((layers, blocks * slot, LANES), f32),
            scratch((layers, devices - 1, slot, LANES), f32),
            scratch((layers, slot, LANES), f32),
            scratch((layers, devices * slot, LANES), f32),
            scratch((layers, half, 3 * depth), bf16),
            scratch((layers, half, 5 * depth), bf16),
            scratch((layers * channels, 4 * LANES), f32),
            scratch((8 * layers * channels, wide), f32),
            scratch((2 * modes_x, 3 * local_rows), bf16),
            scratch((local_rows, 6 * modes_x), bf16),
            scratch((cols, LANES), bf16),
            scratch((6 * MODES_Y, cols), bf16),
            scratch((8, cols), f32),
            scratch((layers, half, LANES), f32),
            scratch((2 * LANES, cols), jnp.int32),
            scratch((2 * channels, LANES), f32),
            scratch((2 * half, 2 * half), bf16),
            scratch((cols, cols), bf16),
            scratch((layers * half, 8 * layers * channels), bf16),
            dma((groups,)),
            dma((groups,)),
            dma((layers, 8)),
            dma((layers, 8)),
            dma((layers, devices - 1)),
            dma((layers, devices - 1)),
            dma((layers, devices - 1)),
            dma((layers, devices - 1)),
        ],
        compiler_params=pltpu.CompilerParams(
            collective_id=0, has_side_effects=True, vmem_limit_bytes=62 * 1024 * 1024
        ),
    )(u, weights, near, far, rtab, ctab, mix, bias)


def solution(mesh):
    sizes = (mesh.shape["gx"], mesh.shape["gy"])

    def on_device(grid_field, spectral_weight, conv_near, conv_far, mix_logits, channel_bias):
        _, channels, local_rows, local_cols = grid_field.shape
        layers = spectral_weight.shape[0]
        share = spectral_weight.shape[-1]
        devices = sizes[0] * sizes[1]
        cells_x, cells_y = local_rows * sizes[0], local_cols * sizes[1]
        modes_x = share * devices // MODES_Y
        per_share = max(share // MODES_Y, 1)
        blocks = modes_x // per_share
        groups = local_rows // GROUP
        planes = local_cols // LANES
        assert share * per_share in (16, 32, 128)
        assert groups * GROUP == local_rows and 8 * groups <= LANES and groups >= 4
        assert cells_x % 4 == 0 and cells_y % 4 == 0
        assert planes * LANES == local_cols and planes in (1, 2, 4)

        mode = jnp.arange(2 * modes_x, dtype=jnp.int32)
        slot = mode % modes_x % blocks * per_share + mode % modes_x // blocks
        row_mode = jnp.where(slot < modes_x // 2, slot, slot + (cells_x - modes_x))
        turn = jnp.where(mode < modes_x, 0, 3 * cells_x // 4)
        index = jnp.arange(local_rows, dtype=jnp.int32)
        row_at = index // GROUP * GROUP + group_order(index % GROUP)
        row_at = row_at + lax.axis_index("gx") * local_rows
        phase = (row_mode[:, None] * row_at[None, :] + turn[:, None]) % cells_x
        rtab = jnp.cos(phase.astype(f32) * (full_turn / cells_x))

        index = jnp.arange(local_cols, dtype=jnp.int32)
        col_at = lax.axis_index("gy") * local_cols + natural_column(index, local_cols)
        lane = jnp.arange(LANES, dtype=jnp.int32)
        turn = jnp.where(lane < MODES_Y, 0, jnp.where(lane < 3 * MODES_Y, 1, 2)) * (cells_y // 4)
        phase = (col_at[:, None] * (lane % MODES_Y)[None, :] + turn[None, :]) % cells_y
        ctab = jnp.cos(phase.astype(f32) * (full_turn / cells_y))

        field = main_call(
            grid_field[0],
            spectral_weight.transpose(0, 2, 3, 1, 4),
            conv_near.transpose(1, 0, 2),
            conv_far.transpose(1, 0, 2),
            rtab, ctab, mix_logits, channel_bias,
            sizes, cells_x * cells_y,
        )
        return restore_call(field, channels)[None]

    in_specs = (
        P(None, None, "gx", "gy"),
        P(None, None, None, None, ("gx", "gy")),
        P(),
        P(),
        P(),
        P(),
    )
    return jax.shard_map(
        on_device,
        mesh=mesh,
        in_specs=in_specs,
        out_specs=P(None, None, "gx", "gy"),
        check_vma=False,
    )
```

```python
import functools
import math

import jax
import jax.numpy as jnp
from jax import lax
from jax.experimental import pallas as pl
from jax.experimental.pallas import tpu as pltpu
from jax.sharding import PartitionSpec as P

full_turn = 2.0 * math.pi
MESH = pl.DeviceIdType.MESH
MODES_Y = 32
GROUP = 16
LANES = 128
HALO = 4
CHUNK = 4
NEAR = (-1, 0, 1)
FAR = (-4, -2, 0, 2, 4)
f32 = jnp.float32
bf16 = jnp.bfloat16


def split_bf16(value):
    high = value.astype(bf16)
    low = (value - high.astype(f32)).astype(bf16)
    return high, low


def group_order(place):
    return place % 8 // 2 * 4 + place % 2 * 2 + place // 8


def iota(shape, dim):
    return lax.broadcasted_iota(jnp.int32, shape, dim)


def natural_order(at, channels):
    return at % channels * GROUP + group_order(at // channels)


def natural_column(at, cols):
    return at % LANES * (cols // LANES) + at // LANES


def matches(left, right):
    return jnp.where(left == right, 1.0, 0.0).astype(bf16)


def restore_kernel(value_ref, out_ref, columns, *, chunk):
    channels, _, cols = out_ref.shape
    whole = channels * GROUP

    @pl.when(pl.program_id(0) == 0)
    def _():
        at = natural_column(iota((cols, LANES), 0), cols)[:, :1]
        columns[...] = matches(at, iota((cols, cols), 1))

    for i in range(chunk):
        value = value_ref[i * whole : (i + 1) * whole, :]
        value = jnp.dot(value, columns[...], preferred_element_type=f32).astype(bf16)
        out_ref[:, i * GROUP : (i + 1) * GROUP, :] = value.reshape(channels, GROUP, cols)


def restore_call(value, channels):
    whole = channels * GROUP
    groups, cols = value.shape[0] // whole, value.shape[1]
    chunk = CHUNK if groups % CHUNK == 0 else 1
    return pl.pallas_call(
        functools.partial(restore_kernel, chunk=chunk),
        grid=(groups // chunk,),
        name="restore",
        in_specs=[pl.BlockSpec((chunk * whole, cols), lambda i: (i, 0))],
        out_specs=pl.BlockSpec((channels, chunk * GROUP, cols), lambda i: (0, i, 0)),
        out_shape=jax.ShapeDtypeStruct((channels, groups * GROUP, cols), bf16),
        scratch_shapes=[pltpu.VMEM((cols, cols), bf16)],
    )(value)


def main_kernel(
    u_ref, sw_ref, near_ref, far_ref, rtab_ref, ctab_ref,
    mix_ref, bias_ref, out_ref,
    ubuf, obuf, nst, fst, conv, lhs, lines, carry, pack, packs, edges, hcol, hrow, hcorner,
    sendbuf, recv, mixed, gath, nw, fw, taps, tall, ftab, itab, fwd, inv, mixb, biasb, code, pairs,
    order, back, columns, stack, pick,
    u_sem, out_sem, halo_send, halo_recv, a2a_send, a2a_recv, gat_send, gat_recv,
    *, sizes, cells, first_part, batch,
):
    gx, gy = sizes
    devices = gx * gy
    layers = sw_ref.shape[0]
    channels, local_rows, cols = ubuf.shape
    pair = 2 * channels
    half = 4 * pair
    whole = 2 * half
    groups = local_rows // GROUP
    planes = cols // LANES
    edge = HALO // planes
    slot = mixed.shape[1]
    blocks = sendbuf.shape[1] // slot
    sharers = devices // blocks
    per_device = 2 * MODES_Y
    modes_x = rtab_ref.shape[0] // 2
    share_rows = modes_x // blocks
    share = sw_ref.shape[-1]
    trim = (pair + 15) // 16 * 16
    my_x, my_y = lax.axis_index("gx"), lax.axis_index("gy")
    me = my_x * gy + my_y

    def place(index):
        return (index // gy, index % gy)

    barrier = pltpu.get_barrier_semaphore()

    @pl.loop(1, devices)
    def _(k):
        pl.semaphore_signal(
            barrier, inc=1, device_id=place((me + k) % devices), device_id_type=MESH
        )

    def u_copy(g):
        rows = pl.ds(pl.multiple_of(g * GROUP, GROUP), GROUP)
        return pltpu.make_async_copy(u_ref.at[:, rows, :], ubuf.at[:, rows, :], u_sem.at[g])

    @pl.loop(0, groups)
    def _(g):
        u_copy(g).start()

    at = natural_order(iota((whole, LANES), 0), channels)[:, :1]
    order[...] = matches(at, iota((whole, whole), 1))
    at = natural_order(iota((8, whole), 1), channels)[:1]
    back[...] = matches(iota((whole, whole), 0), at)
    at = natural_column(iota((8, cols), 1), cols)[:1]
    columns[...] = matches(iota((cols, cols), 0), at)
    at = iota((layers * half, LANES), 0)
    wanted = at % half // channels * (layers * channels) + at % channels * layers + at // half
    stack[...] = matches(wanted[:, :1], iota(stack.shape, 1))

    high, low = split_bf16(rtab_ref[...])
    ftab[...] = jnp.concatenate([high, high, low], axis=1)
    high, low = split_bf16(rtab_ref[...].T)
    itab[...] = jnp.concatenate([high, high, low], axis=1)
    fwd[...] = ctab_ref[...].astype(bf16)
    turned_cols = ctab_ref[...].T[:per_device]
    weight = jnp.where(iota((per_device, cols), 0) % MODES_Y == 0, 1.0, 2.0) / cells
    high, low = split_bf16(turned_cols * weight)
    inv[...] = jnp.concatenate([high, high, low], axis=0)

    exponents = jnp.exp(mix_ref[...])
    mixtures = exponents / jnp.sum(exponents, axis=1, keepdims=True)
    for layer in range(layers):
        for i in range(3):
            at = 3 * layer + i
            mixb[at : at + 1, :] = jnp.broadcast_to(
                mixtures[layer : layer + 1, i : i + 1], (1, cols)
            )
        same = iota((half, channels), 0) % channels == iota((half, channels), 1)
        column = jnp.sum(
            jnp.where(same, bias_ref[layer : layer + 1, :], 0.0), axis=1, keepdims=True
        )
        biasb[layer] = jnp.broadcast_to(column, (half, LANES))

    at, lane_at = iota(code.shape, 0), iota(code.shape, 1)
    plane, lane = lane_at // LANES, lane_at % LANES
    before = planes * (lane - (LANES - edge)) + plane
    after = planes * lane + plane
    code[...] = jnp.where(
        (at < LANES) & (lane >= LANES - edge),
        at - before,
        jnp.where((at >= LANES) & (lane < edge), at - LANES - after, -1),
    )

    pick[...] = matches(code[...], 0)

    def roll_halves(value, amount):
        return jnp.concatenate(
            [pltpu.roll(value[:, i * LANES : (i + 1) * LANES], amount, 1) for i in range(2)], axis=1
        )

    def edge_columns(packed, k):
        turned_back = roll_halves(packed, (LANES - HALO * k) % LANES).astype(bf16)
        return jnp.dot(turned_back, pick[...], preferred_element_type=f32)

    depth = 6 * pair
    wide = (depth + LANES - 1) // LANES * LANES

    def tap_rows(taps_ref):
        count = taps_ref.shape[2]
        for o in range(channels):
            taps[layers * o : layers * (o + 1), :count] = taps_ref[o].astype(f32)
        return taps[:, :count].astype(bf16)

    rows_of = layers * channels

    def spread(out_ref, index):
        stacked = tall[...].astype(bf16)
        full = jnp.dot(stack[...], stacked, preferred_element_type=f32).astype(bf16)
        return [full[layer * half : (layer + 1) * half, :depth] for layer in range(layers)]

    def emit(out_ref, pieces):
        for layer in range(layers):
            out_ref[layer] = jnp.concatenate([piece[layer] for piece in pieces], axis=1)

    def spread_taps():
        source = tap_rows(far_ref)
        count = far_ref.shape[2]
        target = iota((count, wide), 1)
        base = jnp.where(
            target < 5 * channels,
            target // channels * (5 * channels) + target % channels,
            -count,
        )
        base = iota((count, wide), 0) - base
        pieces = []
        for column in range(5):
            chosen = matches(base, column * channels)
            block = jnp.dot(source, chosen, preferred_element_type=f32)
            for row in range(8):
                tall[rows_of * row : rows_of * (row + 1), :] = (
                    pltpu.roll(block, channels * row, 1) if row else block
                )
            pieces.append(spread(fw, column))
        emit(fw, pieces)

        source = tap_rows(near_ref)
        count = near_ref.shape[2]
        target = iota((count, wide), 1)
        spot, channel = target // channels, target % channels
        where_row = {-1: 1, 0: 2, 1: 4, 2: 3, 3: 5, 4: 6}
        bases = []
        for row in range(4):
            tap = jnp.full(target.shape, -count, jnp.int32)
            for step in range(3):
                tap = jnp.where(
                    spot == where_row[row + step - 1], step * 3 * channels + channel, tap
                )
            bases.append(iota((count, wide), 0) - tap)
        pieces = []
        for column in range(3):
            for row in range(4):
                chosen = matches(bases[row], column * channels)
                block = jnp.dot(source, chosen, preferred_element_type=f32)
                for quad in range(2):
                    full_row = 4 * quad + row
                    index = full_row % 2 * 4 + full_row // 2
                    tall[rows_of * index : rows_of * (index + 1), :] = (
                        pltpu.roll(block, 4 * channels, 1) if quad else block
                    )
            pieces.append(spread(nw, column))
        emit(nw, pieces)

    def near_edges(value):
        low_lanes = iota((value.shape[0], LANES), 1) < LANES // 2
        return jnp.where(low_lanes, value[:, :LANES], value[:, cols - LANES :])

    def store_rows(g, even, odd, side):
        at = slice(side * cols, (side + 1) * cols)
        old_even, old_odd = carry[0, :, at], carry[1, :, at]
        q = [(even[i * pair : (i + 1) * pair], odd[i * pair : (i + 1) * pair]) for i in range(4)]
        near_rows = [old_odd]
        for i in range(4):
            near_rows.append(q[i][0])
            if i < 3:
                near_rows.append(q[i][1])
        near_rows = jnp.concatenate(near_rows, axis=0)
        near_at = pl.ds(pl.multiple_of(g * whole, whole), whole)
        if side:
            nst[near_at, cols:] = near_edges(near_rows).astype(bf16)
        else:
            nst[near_at, :cols] = near_rows.astype(bf16)
        row = pl.ds(pl.multiple_of(g * half, half), half)
        fst[0, row, at] = jnp.concatenate([old_even, even[: 3 * pair]], axis=0).astype(bf16)
        fst[1, row, at] = jnp.concatenate([old_odd, odd[: 3 * pair]], axis=0).astype(bf16)
        carry[0, :, at] = q[3][0]
        carry[1, :, at] = q[3][1]

    def ingest(g, value):
        full = value.astype(f32)
        even, odd = full[:half], full[half:]
        store_rows(g, even, odd, 0)
        lines[pl.ds(pl.multiple_of(g * whole, whole), whole), :] = jnp.dot(
            value, fwd[...], preferred_element_type=f32
        )
        total = pack[...]
        for p in range(2):
            found = lax.dot_general(
                value[p * half : (p + 1) * half],
                pick[...],
                (((1,), (1,)), ((), ())),
                preferred_element_type=f32,
            )
            total = total + roll_halves(found, HALO * (2 * g + p))
        pack[...] = total

    carry[...] = jnp.zeros_like(carry)
    pack[...] = jnp.zeros_like(pack)

    @pl.loop(0, groups // 2)
    def _(b):
        values = []
        for i in range(2):
            u_copy(2 * b + i).wait()
        for i in range(2):
            at = pl.ds(pl.multiple_of((2 * b + i) * GROUP, GROUP), GROUP)
            slab = ubuf[:, at, :].reshape(whole, cols)
            values.append(jnp.dot(order[...], slab, preferred_element_type=f32).astype(bf16))
        values = [
            jnp.dot(value, columns[...], preferred_element_type=f32).astype(bf16)
            for value in values
        ]
        for i in range(2):
            ingest(2 * b + i, values[i])

    pl.semaphore_wait(barrier, devices - 1)

    up, down = (my_x + gx - 1) % gx, (my_x + 1) % gx
    left, right = (my_y + gy - 1) % gy, (my_y + 1) % gy

    def halo_copies(layer):
        def copy(i, src, dst, target):
            return pltpu.make_async_remote_copy(
                src_ref=src, dst_ref=dst, send_sem=halo_send.at[layer, i],
                recv_sem=halo_recv.at[layer, i], device_id=target, device_id_type=MESH,
            )

        mine, beside = packs.at[layer], hcol.at[layer]
        above, below = hcorner.at[layer, 0], hcorner.at[layer, 1]
        lasts, firsts = slice(0, LANES), slice(LANES, 2 * LANES)
        head, tail = slice(0, trim), slice(half - trim, half)
        return [
            copy(0, mine.at[:, firsts], beside.at[:, firsts], (my_x, left)),
            copy(1, mine.at[:, lasts], beside.at[:, lasts], (my_x, right)),
            copy(2, edges.at[layer, 0], hrow.at[layer, 1], (up, my_y)),
            copy(3, edges.at[layer, 1], hrow.at[layer, 0], (down, my_y)),
            copy(4, mine.at[head, firsts], below.at[:, firsts], (up, left)),
            copy(5, mine.at[tail, firsts], above.at[:, firsts], (down, left)),
            copy(6, mine.at[head, lasts], below.at[:, lasts], (up, right)),
            copy(7, mine.at[tail, lasts], above.at[:, lasts], (down, right)),
        ]

    def a2a_copy(layer, k):
        target = (me + k) % devices
        return pltpu.make_async_remote_copy(
            src_ref=sendbuf.at[layer, pl.ds(target // sharers * slot, slot)],
            dst_ref=recv.at[layer, k - 1],
            send_sem=a2a_send.at[layer, k - 1],
            recv_sem=a2a_recv.at[layer, k - 1],
            device_id=place(target),
            device_id_type=MESH,
        )

    def gather_copy(layer, k):
        return pltpu.make_async_remote_copy(
            src_ref=mixed.at[layer],
            dst_ref=gath.at[layer, pl.ds(me * slot, slot)],
            send_sem=gat_send.at[layer, k - 1],
            recv_sem=gat_recv.at[layer, k - 1],
            device_id=place((me + k) % devices),
            device_id_type=MESH,
        )

    def turned(value):
        return jnp.where(
            (iota(value.shape, 1) // MODES_Y) % 2 == 1,
            pltpu.roll(value, MODES_Y, 1),
            -pltpu.roll(value, LANES - MODES_Y, 1),
        )

    def triple(value):
        high, low = split_bf16(value)
        return jnp.concatenate([high, low, high], axis=0)

    def row_transform(layer):
        @pl.loop(0, channels // batch, unroll=5 if channels // batch % 5 == 0 else 1)
        def _(b):
            parts = [
                triple(lines[pl.ds(b * batch + i, local_rows, stride=channels), :])
                for i in range(batch)
            ]
            result = jnp.dot(
                ftab[...], jnp.concatenate(parts, axis=1), preferred_element_type=f32
            )
            for i in range(batch):
                both = result[:, i * LANES : (i + 1) * LANES]
                total = both[:modes_x] + pltpu.roll(both[modes_x:], per_device, 1)
                block = total
                if share_rows == 2:
                    block = jnp.where(
                        iota((blocks, LANES), 1) < per_device,
                        total[:blocks],
                        pltpu.roll(total[blocks:], per_device, 1),
                    )
                sendbuf[layer, pl.ds(b * batch + i, blocks, stride=slot), :] = block

    def mix_modes(layer):
        own = sendbuf[layer, pl.ds(pl.multiple_of(me // sharers * slot, 8), slot), :]

        @pl.loop(1, devices)
        def _(k):
            a2a_copy(layer, k).wait_recv()

        own = own + jnp.sum(recv[layer], axis=0)
        crossed = turned(own)
        is_real = iota((2 * channels, LANES), 0) % 2 == 0

        def spread_lanes(part):
            if share_rows == 1:
                tiled = jnp.concatenate([part] * (LANES // share), axis=1)
                at = iota(tiled.shape, 1) // share
                return jnp.where(at % sharers == me % sharers, tiled, 0.0)
            pieces = []
            for j in range(share_rows):
                piece = part[:, j * MODES_Y : (j + 1) * MODES_Y]
                pieces += [piece, piece]
            return jnp.concatenate(pieces, axis=1)

        total = jnp.zeros((2 * channels, LANES), f32)
        for c in range(channels):
            weights = spread_lanes(sw_ref[layer, c].reshape(2 * channels, share))
            total = total + weights * jnp.where(is_real, own[c : c + 1], crossed[c : c + 1])
        pairs[...] = total
        total = pairs[pl.ds(0, channels, stride=2), :] + pairs[pl.ds(1, channels, stride=2), :]
        total = total * mixb[3 * layer : 3 * layer + 1, :LANES]
        mixed[layer, :channels, :] = total
        gath[layer, pl.ds(pl.multiple_of(me * slot, 8), channels), :] = total

        @pl.loop(1, devices)
        def _(k):
            gather_copy(layer, k).start()

    def inverse_rows(layer):
        @pl.loop(1, devices)
        def _(k):
            gather_copy(layer, k).wait_recv()

        @pl.loop(0, channels // batch, unroll=5 if channels // batch % 5 == 0 else 1)
        def _(b):
            parts = []
            for i in range(batch):
                o = b * batch + i
                block = gath[layer, pl.ds(o, blocks, stride=slot * sharers), :]
                for j in range(1, sharers):
                    block = block + gath[layer, pl.ds(j * slot + o, blocks, stride=slot * sharers), :]
                cross = turned(block)
                stack = [block, cross]
                if share_rows == 2:
                    stack = [block, pltpu.roll(block, per_device, 1)]
                    stack += [cross, pltpu.roll(cross, per_device, 1)]
                parts.append(triple(jnp.concatenate(stack, axis=0)))
            result = jnp.dot(
                itab[...], jnp.concatenate(parts, axis=1), preferred_element_type=f32
            )
            for i in range(batch):
                lhs[pl.ds(b * batch + i, local_rows, stride=channels), :] = result[
                    :, i * LANES : (i + 1) * LANES
                ]

    def conv_groups(layer, g, count):
        def window(rows, shifts, beside):
            own = [rows[:, s * LANES : (s + 1) * LANES] for s in range(planes)]
            at = iota((rows.shape[0], LANES), 1)
            known = {}

            def piece(s, d):
                q = s + d
                plane, move = q % planes, q // planes
                if (plane, move) not in known:
                    value = own[plane]
                    if move > 0:
                        value = jnp.where(at < move, beside(plane), value)
                    if move < 0:
                        value = jnp.where(at >= LANES + move, beside(plane), value)
                    if move:
                        value = pltpu.roll(value, (-move) % LANES, 1)
                    known[plane, move] = value
                return known[plane, move]

            return [jnp.concatenate([piece(s, d) for s in range(planes)], axis=1) for d in shifts]

        rows = nst[pl.ds(pl.multiple_of(g * whole, whole), (2 * count - 1) * half + depth), :]
        near_columns = window(rows, NEAR, lambda plane: rows[:, cols:])
        far_columns = []
        for p in range(2):
            rows = fst[p, pl.ds(pl.multiple_of(g * half, half), (count - 1) * half + depth), :]
            far_columns.append(
                window(rows, FAR, lambda s: rows[:, cols + s * LANES : cols + (s + 1) * LANES])
            )
        bias = jnp.concatenate([biasb[layer]] * planes, axis=1)

        def apply(weights, parts, start):
            columns = jnp.concatenate([part[start : start + depth] for part in parts], axis=0)
            return jnp.dot(weights, columns, preferred_element_type=f32)

        for i in range(count):
            near = [apply(nw[layer], near_columns, (2 * i + h) * half) for h in range(2)]
            parts = []
            for p in range(2):
                far = apply(fw[layer], far_columns[p], i * half)
                side = slice(p * 2 * pair, (p + 1) * 2 * pair)
                close = jnp.concatenate([near[0][side], near[1][side]], axis=0)
                total = (
                    mixb[3 * layer + 1 : 3 * layer + 2, :] * close
                    + mixb[3 * layer + 2 : 3 * layer + 3, :] * far
                    + bias
                )
                parts.append(total)
            conv[pl.ds(pl.multiple_of((g + i) * whole, whole), whole), :] = jnp.concatenate(
                parts, axis=0
            )

    def out_copy(g):
        rows = pl.ds(pl.multiple_of(g * whole, whole), whole)
        return pltpu.make_async_copy(obuf.at[rows], out_ref.at[rows], out_sem.at[g])

    def finish_pair(layer, b):
        spots = [pl.ds(pl.multiple_of((2 * b + i) * whole, whole), whole) for i in range(2)]
        values = []
        for at in spots:
            high, low = split_bf16(lhs[at, :per_device])
            spectral = jnp.dot(
                jnp.concatenate([high, low, high], axis=1), inv[...], preferred_element_type=f32
            )
            value = conv[at, :] + spectral
            value = value * 0.5 * (1.0 + lax.erf(value * (0.5**0.5)))
            values.append(value.astype(bf16))
        if layer + 1 < layers:
            for i in range(2):
                ingest(2 * b + i, values[i])
        else:
            values = [
                jnp.dot(back[...], value, preferred_element_type=f32).astype(bf16)
                for value in values
            ]
            for i in range(2):
                obuf[spots[i], :] = values[i]
            for i in range(2):
                out_copy(2 * b + i).start()

    for layer in range(layers):
        packs[layer] = pack[...].astype(bf16)
        tops = [fst[p, : 2 * pair, :cols].astype(f32)[pair:] for p in range(2)]
        edges[layer, 0] = jnp.concatenate(tops, axis=0).astype(bf16)
        bottoms = [carry[p, :, :cols] for p in range(2)]
        edges[layer, 1] = jnp.concatenate(bottoms, axis=0).astype(bf16)
        halos = halo_copies(layer)
        for copy in halos:
            copy.start()
        row_transform(layer)

        @pl.loop(1, devices)
        def _(k):
            a2a_copy(layer, k).start()

        if layer == 0:
            spread_taps()
        for copy in halos[:2]:
            copy.wait_recv()
        carry[:, :, cols:] = jnp.zeros((2, pair, cols), f32)
        pack[...] = hcol[layer].astype(f32)

        @pl.loop(0, groups, unroll=2)
        def _(g):
            parts = [edge_columns(pack[...], 2 * g + p) for p in range(2)]
            store_rows(g, parts[0], parts[1], 1)

        twos = (groups - 2) // 2
        cut = first_part * twos // 14

        @pl.loop(0, cut)
        def _(b):
            conv_groups(layer, 1 + 2 * b, 2)

        mix_modes(layer)

        @pl.loop(cut, twos)
        def _(b):
            conv_groups(layer, 1 + 2 * b, 2)

        for copy in halos[2:]:
            copy.wait_recv()

        def halo_rows(side):
            k = 0 if side else 2 * (groups - 1)
            main = hrow[layer, side].astype(f32)
            out = []
            for p in range(2):
                corner = edge_columns(hcorner[layer, side].astype(f32), k + p)
                corner = corner[:pair] if side else corner[trim - pair :]
                out.append((main[p * pair : (p + 1) * pair], corner))
            return out

        above, below = halo_rows(0), halo_rows(1)
        first = slice(0, 2 * pair)

        def patch(rows, halo):
            return jnp.concatenate([halo, rows.astype(f32)[pair:]], axis=0).astype(bf16)

        nst[first, :cols] = patch(nst[first, :cols], above[1][0])
        nst[first, cols:] = patch(nst[first, cols:], near_edges(above[1][1]))
        end = groups * whole
        last = slice(end, end + 2 * pair)
        nst[last, :cols] = jnp.concatenate([carry[1, :, :cols], below[0][0]], axis=0).astype(bf16)
        nst[last, cols:] = near_edges(
            jnp.concatenate([carry[1, :, cols:], below[0][1]], axis=0)
        ).astype(bf16)
        end = groups * half
        last = slice(end, end + 2 * pair)
        for p in range(2):
            for side in range(2):
                at = slice(side * cols, (side + 1) * cols)
                fst[p, first, at] = patch(fst[p, first, at], above[p][side])
                fst[p, last, at] = jnp.concatenate(
                    [carry[p, :, at], below[p][side]], axis=0
                ).astype(bf16)

        @pl.loop(0, 2)
        def _(i):
            conv_groups(layer, i * (groups - 1), 1)

        inverse_rows(layer)
        carry[...] = jnp.zeros_like(carry)
        pack[...] = jnp.zeros_like(pack)

        @pl.loop(0, groups // 2)
        def _(b):
            finish_pair(layer, b)

        for copy in halos:
            copy.wait_send()

        @pl.loop(1, devices)
        def _(k):
            a2a_copy(layer, k).wait_send()
            gather_copy(layer, k).wait_send()

    @pl.loop(0, groups)
    def _(g):
        out_copy(g).wait()


def main_call(u, weights, near, far, rtab, ctab, mix, bias, sizes, cells):
    channels, local_rows, cols = u.shape
    layers = weights.shape[0]
    devices = sizes[0] * sizes[1]
    pair = 2 * channels
    half = 4 * pair
    slot = (channels + 7) // 8 * 8
    blocks = devices * min(weights.shape[-1], MODES_Y) // MODES_Y
    groups = local_rows // GROUP
    modes_x = rtab.shape[0] // 2
    depth = 6 * pair
    wide = (depth + LANES - 1) // LANES * LANES
    trim = (pair + 15) // 16 * 16
    vmem = pl.BlockSpec(memory_space=pltpu.VMEM)
    anywhere = pl.BlockSpec(memory_space=pl.ANY)
    dma = pltpu.SemaphoreType.DMA
    scratch = pltpu.VMEM
    return pl.pallas_call(
        functools.partial(
            main_kernel, sizes=sizes, cells=cells, first_part=6,
            batch=4 if channels % 4 == 0 else 1,
        ),
        name="operator",
        out_shape=jax.ShapeDtypeStruct((groups * 2 * half, cols), bf16),
        in_specs=[anywhere] + [vmem] * 7,
        out_specs=anywhere,
        scratch_shapes=[
            scratch((channels, local_rows, cols), bf16),
            scratch((groups * 2 * half, cols), bf16),
            scratch((groups * 2 * half + 2 * pair, cols + LANES), bf16),
            scratch((2, groups * half + 2 * pair, 2 * cols), bf16),
            scratch((groups * 2 * half, cols), f32),
            scratch((groups * 2 * half, LANES), f32),
            scratch((groups * 2 * half, LANES), f32),
            scratch((2, pair, 2 * cols), f32),
            scratch((half, 2 * LANES), f32),
            scratch((layers, half, 2 * LANES), bf16),
            scratch((layers, 2, 2 * pair, cols), bf16),
            scratch((layers, half, 2 * LANES), bf16),
            scratch((layers, 2, 2 * pair, cols), bf16),
            scratch((layers, 2, trim, 2 * LANES), bf16),
            scratch((layers, blocks * slot, LANES), f32),
            scratch((layers, devices - 1, slot, LANES), f32),
            scratch((layers, slot, LANES), f32),
            scratch((layers, devices * slot, LANES), f32),
            scratch((layers, half, 3 * depth), bf16),
            scratch((layers, half, 5 * depth), bf16),
            scratch((layers * channels, 4 * LANES), f32),
            scratch((8 * layers * channels, wide), f32),
            scratch((2 * modes_x, 3 * local_rows), bf16),
            scratch((local_rows, 6 * modes_x), bf16),
            scratch((cols, LANES), bf16),
            scratch((6 * MODES_Y, cols), bf16),
            scratch((8, cols), f32),
            scratch((layers, half, LANES), f32),
            scratch((2 * LANES, cols), jnp.int32),
            scratch((2 * channels, LANES), f32),
            scratch((2 * half, 2 * half), bf16),
            scratch((2 * half, 2 * half), bf16),
            scratch((cols, cols), bf16),
            scratch((layers * half, 8 * layers * channels), bf16),
            scratch((2 * LANES, cols), bf16),
            dma((groups,)),
            dma((groups,)),
            dma((layers, 8)),
            dma((layers, 8)),
            dma((layers, devices - 1)),
            dma((layers, devices - 1)),
            dma((layers, devices - 1)),
            dma((layers, devices - 1)),
        ],
        compiler_params=pltpu.CompilerParams(
            collective_id=0, has_side_effects=True, vmem_limit_bytes=62 * 1024 * 1024
        ),
    )(u, weights, near, far, rtab, ctab, mix, bias)


def solution(mesh):
    sizes = (mesh.shape["gx"], mesh.shape["gy"])

    def on_device(grid_field, spectral_weight, conv_near, conv_far, mix_logits, channel_bias):
        _, channels, local_rows, local_cols = grid_field.shape
        layers = spectral_weight.shape[0]
        share = spectral_weight.shape[-1]
        devices = sizes[0] * sizes[1]
        cells_x, cells_y = local_rows * sizes[0], local_cols * sizes[1]
        modes_x = share * devices // MODES_Y
        per_share = max(share // MODES_Y, 1)
        blocks = modes_x // per_share
        groups = local_rows // GROUP
        planes = local_cols // LANES
        assert share * per_share in (16, 32, 128)
        assert groups * GROUP == local_rows and 8 * groups <= LANES and groups >= 4
        assert groups % 2 == 0
        assert cells_x % 4 == 0 and cells_y % 4 == 0
        assert planes * LANES == local_cols and planes in (1, 2, 4)

        mode = jnp.arange(2 * modes_x, dtype=jnp.int32)
        slot = mode % modes_x % blocks * per_share + mode % modes_x // blocks
        row_mode = jnp.where(slot < modes_x // 2, slot, slot + (cells_x - modes_x))
        turn = jnp.where(mode < modes_x, 0, 3 * cells_x // 4)
        index = jnp.arange(local_rows, dtype=jnp.int32)
        row_at = index // GROUP * GROUP + group_order(index % GROUP)
        row_at = row_at + lax.axis_index("gx") * local_rows
        phase = (row_mode[:, None] * row_at[None, :] + turn[:, None]) % cells_x
        rtab = jnp.cos(phase.astype(f32) * (full_turn / cells_x))

        index = jnp.arange(local_cols, dtype=jnp.int32)
        col_at = lax.axis_index("gy") * local_cols + natural_column(index, local_cols)
        lane = jnp.arange(LANES, dtype=jnp.int32)
        turn = jnp.where(lane < MODES_Y, 0, jnp.where(lane < 3 * MODES_Y, 1, 2)) * (cells_y // 4)
        phase = (col_at[:, None] * (lane % MODES_Y)[None, :] + turn[None, :]) % cells_y
        ctab = jnp.cos(phase.astype(f32) * (full_turn / cells_y))

        field = main_call(
            grid_field[0],
            spectral_weight.transpose(0, 2, 3, 1, 4),
            conv_near.transpose(1, 0, 2),
            conv_far.transpose(1, 0, 2),
            rtab, ctab, mix_logits, channel_bias,
            sizes, cells_x * cells_y,
        )
        return restore_call(field, channels)[None]

    in_specs = (
        P(None, None, "gx", "gy"),
        P(None, None, None, None, ("gx", "gy")),
        P(),
        P(),
        P(),
        P(),
    )
    return jax.shard_map(
        on_device,
        mesh=mesh,
        in_specs=in_specs,
        out_specs=P(None, None, "gx", "gy"),
        check_vma=False,
    )
```

```python
import functools
import math

import jax
import jax.numpy as jnp
from jax import lax
from jax.experimental import pallas as pl
from jax.experimental.pallas import tpu as pltpu
from jax.sharding import PartitionSpec as P

full_turn = 2.0 * math.pi
MESH = pl.DeviceIdType.MESH
MODES_Y = 32
GROUP = 16
LANES = 128
HALO = 4
CHUNK = 4
NEAR = (-1, 0, 1)
FAR = (-4, -2, 0, 2, 4)
f32 = jnp.float32
bf16 = jnp.bfloat16


def split_bf16(value):
    high = value.astype(bf16)
    low = (value - high.astype(f32)).astype(bf16)
    return high, low


def group_order(place):
    return place % 8 // 2 * 4 + place % 2 * 2 + place // 8


def iota(shape, dim):
    return lax.broadcasted_iota(jnp.int32, shape, dim)


def natural_order(at, channels):
    return at % channels * GROUP + group_order(at // channels)


def natural_column(at, cols):
    return at % LANES * (cols // LANES) + at // LANES


def matches(left, right):
    return jnp.where(left == right, 1.0, 0.0).astype(bf16)


def restore_kernel(value_ref, out_ref, columns, *, chunk):
    channels, _, cols = out_ref.shape
    whole = channels * GROUP

    @pl.when(pl.program_id(0) == 0)
    def _():
        at = natural_column(iota((cols, LANES), 0), cols)[:, :1]
        columns[...] = matches(at, iota((cols, cols), 1))

    for i in range(chunk):
        value = value_ref[i * whole : (i + 1) * whole, :]
        value = jnp.dot(value, columns[...], preferred_element_type=f32).astype(bf16)
        out_ref[:, i * GROUP : (i + 1) * GROUP, :] = value.reshape(channels, GROUP, cols)


def restore_call(value, channels):
    whole = channels * GROUP
    groups, cols = value.shape[0] // whole, value.shape[1]
    chunk = CHUNK if groups % CHUNK == 0 else 1
    return pl.pallas_call(
        functools.partial(restore_kernel, chunk=chunk),
        grid=(groups // chunk,),
        name="restore",
        in_specs=[pl.BlockSpec((chunk * whole, cols), lambda i: (i, 0))],
        out_specs=pl.BlockSpec((channels, chunk * GROUP, cols), lambda i: (0, i, 0)),
        out_shape=jax.ShapeDtypeStruct((channels, groups * GROUP, cols), bf16),
        scratch_shapes=[pltpu.VMEM((cols, cols), bf16)],
    )(value)


def main_kernel(
    u_ref, sw_ref, near_ref, far_ref, rtab_ref, ctab_ref,
    mix_ref, bias_ref, out_ref,
    ubuf, obuf, nst, fst, conv, lhs, lines, carry, pack, packs, edges, hcol, hrow, hcorner,
    sendbuf, recv, mixed, gath, nw, fw, taps, tall, ftab, itab, fwd, inv, mixb, biasb, code, pairs,
    order, back, columns, stack, pick,
    u_sem, out_sem, halo_send, halo_recv, a2a_send, a2a_recv, gat_send, gat_recv,
    *, sizes, cells, first_part, batch,
):
    gx, gy = sizes
    devices = gx * gy
    layers = sw_ref.shape[0]
    channels, local_rows, cols = ubuf.shape
    pair = 2 * channels
    half = 4 * pair
    whole = 2 * half
    groups = local_rows // GROUP
    planes = cols // LANES
    edge = HALO // planes
    slot = mixed.shape[1]
    blocks = sendbuf.shape[1] // slot
    sharers = devices // blocks
    per_device = 2 * MODES_Y
    modes_x = rtab_ref.shape[0] // 2
    share_rows = modes_x // blocks
    share = sw_ref.shape[-1]
    trim = (pair + 15) // 16 * 16
    my_x, my_y = lax.axis_index("gx"), lax.axis_index("gy")
    me = my_x * gy + my_y

    def place(index):
        return (index // gy, index % gy)

    barrier = pltpu.get_barrier_semaphore()

    def u_copy(g):
        rows = pl.ds(pl.multiple_of(g * GROUP, GROUP), GROUP)
        return pltpu.make_async_copy(u_ref.at[:, rows, :], ubuf.at[:, rows, :], u_sem.at[g])

    @pl.loop(0, groups)
    def _(g):
        u_copy(g).start()

    @pl.loop(1, devices)
    def _(k):
        pl.semaphore_signal(
            barrier, inc=1, device_id=place((me + k) % devices), device_id_type=MESH
        )

    at = natural_order(iota((whole, LANES), 0), channels)[:, :1]
    order[...] = matches(at, iota((whole, whole), 1))
    at = natural_order(iota((8, whole), 1), channels)[:1]
    back[...] = matches(iota((whole, whole), 0), at)
    at = natural_column(iota((8, cols), 1), cols)[:1]
    columns[...] = matches(iota((cols, cols), 0), at)
    at = iota((layers * half, LANES), 0)
    wanted = at % half // channels * (layers * channels) + at % channels * layers + at // half
    stack[...] = matches(wanted[:, :1], iota(stack.shape, 1))

    high, low = split_bf16(rtab_ref[...])
    ftab[...] = jnp.concatenate([high, high, low], axis=1)
    high, low = split_bf16(rtab_ref[...].T)
    itab[...] = jnp.concatenate([high, high, low], axis=1)
    turned_cols = ctab_ref[...]
    cosine, sine = turned_cols[:MODES_Y], turned_cols[MODES_Y:]
    fwd[...] = jnp.concatenate([cosine, sine, sine, -cosine], axis=0).T.astype(bf16)
    weight = jnp.where(iota((per_device, cols), 0) % MODES_Y == 0, 1.0, 2.0) / cells
    high, low = split_bf16(turned_cols * weight)
    inv[...] = jnp.concatenate([high, high, low], axis=0)

    exponents = jnp.exp(mix_ref[...])
    mixtures = exponents / jnp.sum(exponents, axis=1, keepdims=True)
    for layer in range(layers):
        for i in range(3):
            at = 3 * layer + i
            mixb[at : at + 1, :] = jnp.broadcast_to(
                mixtures[layer : layer + 1, i : i + 1], (1, cols)
            )
        same = iota((half, channels), 0) % channels == iota((half, channels), 1)
        column = jnp.sum(
            jnp.where(same, bias_ref[layer : layer + 1, :], 0.0), axis=1, keepdims=True
        )
        biasb[layer] = jnp.broadcast_to(column, (half, LANES))

    at, lane_at = iota(code.shape, 0), iota(code.shape, 1)
    plane, lane = lane_at // LANES, lane_at % LANES
    before = planes * (lane - (LANES - edge)) + plane
    after = planes * lane + plane
    code[...] = jnp.where(
        (at < LANES) & (lane >= LANES - edge),
        at - before,
        jnp.where((at >= LANES) & (lane < edge), at - LANES - after, -1),
    )

    pick[...] = matches(code[...], 0)

    def roll_halves(value, amount):
        return jnp.concatenate(
            [pltpu.roll(value[:, i * LANES : (i + 1) * LANES], amount, 1) for i in range(2)], axis=1
        )

    def edge_columns(packed, k):
        turned_back = roll_halves(packed, (LANES - HALO * k) % LANES).astype(bf16)
        return jnp.dot(turned_back, pick[...], preferred_element_type=f32)

    depth = 6 * pair
    wide = (depth + LANES - 1) // LANES * LANES

    def tap_rows(taps_ref):
        count = taps_ref.shape[2]
        for o in range(channels):
            taps[layers * o : layers * (o + 1), :count] = taps_ref[o].astype(f32)
        return taps[:, :count].astype(bf16)

    rows_of = layers * channels

    def spread(out_ref, index):
        stacked = tall[...].astype(bf16)
        full = jnp.dot(stack[...], stacked, preferred_element_type=f32).astype(bf16)
        return [full[layer * half : (layer + 1) * half, :depth] for layer in range(layers)]

    def emit(out_ref, pieces):
        for layer in range(layers):
            out_ref[layer] = jnp.concatenate([piece[layer] for piece in pieces], axis=1)

    def spread_taps():
        source = tap_rows(far_ref)
        count = far_ref.shape[2]
        target = iota((count, wide), 1)
        base = jnp.where(
            target < 5 * channels,
            target // channels * (5 * channels) + target % channels,
            -count,
        )
        base = iota((count, wide), 0) - base
        pieces = []
        for column in range(5):
            chosen = matches(base, column * channels)
            block = jnp.dot(source, chosen, preferred_element_type=f32)
            for row in range(8):
                tall[rows_of * row : rows_of * (row + 1), :] = (
                    pltpu.roll(block, channels * row, 1) if row else block
                )
            pieces.append(spread(fw, column))
        emit(fw, pieces)

        source = tap_rows(near_ref)
        count = near_ref.shape[2]
        target = iota((count, wide), 1)
        spot, channel = target // channels, target % channels
        where_row = {-1: 1, 0: 2, 1: 4, 2: 3, 3: 5, 4: 6}
        bases = []
        for row in range(4):
            tap = jnp.full(target.shape, -count, jnp.int32)
            for step in range(3):
                tap = jnp.where(
                    spot == where_row[row + step - 1], step * 3 * channels + channel, tap
                )
            bases.append(iota((count, wide), 0) - tap)
        pieces = []
        for column in range(3):
            for row in range(4):
                chosen = matches(bases[row], column * channels)
                block = jnp.dot(source, chosen, preferred_element_type=f32)
                for quad in range(2):
                    full_row = 4 * quad + row
                    index = full_row % 2 * 4 + full_row // 2
                    tall[rows_of * index : rows_of * (index + 1), :] = (
                        pltpu.roll(block, 4 * channels, 1) if quad else block
                    )
            pieces.append(spread(nw, column))
        emit(nw, pieces)

    def near_edges(value):
        low_lanes = iota((value.shape[0], LANES), 1) < LANES // 2
        return jnp.where(low_lanes, value[:, :LANES], value[:, cols - LANES :])

    def store_groups(first, values, side):
        at = slice(side * cols, (side + 1) * cols)
        old = carry[0, :, at], carry[1, :, at]
        for i, (even, odd) in enumerate(values):
            old = store_rows(first + i, even, odd, old, side)
        carry[0, :, at], carry[1, :, at] = old

    def store_rows(g, even, odd, old, side):
        at = slice(side * cols, (side + 1) * cols)
        old_even, old_odd = old
        q = [(even[i * pair : (i + 1) * pair], odd[i * pair : (i + 1) * pair]) for i in range(4)]
        near_rows = [old_odd]
        for i in range(4):
            near_rows.append(q[i][0])
            if i < 3:
                near_rows.append(q[i][1])
        near_rows = jnp.concatenate(near_rows, axis=0)
        near_at = pl.ds(pl.multiple_of(g * whole, whole), whole)
        if side:
            nst[near_at, cols:] = near_edges(near_rows).astype(bf16)
        else:
            nst[near_at, :cols] = near_rows.astype(bf16)
        row = pl.ds(pl.multiple_of(g * half, half), half)
        fst[0, row, at] = jnp.concatenate([old_even, even[: 3 * pair]], axis=0).astype(bf16)
        fst[1, row, at] = jnp.concatenate([old_odd, odd[: 3 * pair]], axis=0).astype(bf16)
        return q[3]

    def ingest(first, values):
        total = pack[...]
        sums, parts = [], []
        for i, value in enumerate(values):
            sums.append(jnp.dot(value, fwd[...], preferred_element_type=f32))
            for p in range(2):
                found = lax.dot_general(
                    value[p * half : (p + 1) * half],
                    pick[...],
                    (((1,), (1,)), ((), ())),
                    preferred_element_type=f32,
                )
                total = total + roll_halves(found, HALO * (2 * (first + i) + p))
            full = value.astype(f32)
            parts.append((full[:half], full[half:]))
        pack[...] = total
        for i, found in enumerate(sums):
            lines[pl.ds(pl.multiple_of((first + i) * whole, whole), whole), :] = found
        store_groups(first, parts, 0)

    carry[...] = jnp.zeros_like(carry)
    pack[...] = jnp.zeros_like(pack)

    @pl.loop(0, groups // 2)
    def _(b):
        values = []
        for i in range(2):
            u_copy(2 * b + i).wait()
        for i in range(2):
            at = pl.ds(pl.multiple_of((2 * b + i) * GROUP, GROUP), GROUP)
            slab = ubuf[:, at, :].reshape(whole, cols)
            values.append(jnp.dot(order[...], slab, preferred_element_type=f32).astype(bf16))
        values = [
            jnp.dot(value, columns[...], preferred_element_type=f32).astype(bf16)
            for value in values
        ]
        ingest(2 * b, values)

    pl.semaphore_wait(barrier, devices - 1)

    up, down = (my_x + gx - 1) % gx, (my_x + 1) % gx
    left, right = (my_y + gy - 1) % gy, (my_y + 1) % gy

    def halo_copies(layer):
        def copy(i, src, dst, target):
            return pltpu.make_async_remote_copy(
                src_ref=src, dst_ref=dst, send_sem=halo_send.at[layer, i],
                recv_sem=halo_recv.at[layer, i], device_id=target, device_id_type=MESH,
            )

        mine, beside = packs.at[layer], hcol.at[layer]
        above, below = hcorner.at[layer, 0], hcorner.at[layer, 1]
        lasts, firsts = slice(0, LANES), slice(LANES, 2 * LANES)
        head, tail = slice(0, trim), slice(half - trim, half)
        return [
            copy(0, mine.at[:, firsts], beside.at[:, firsts], (my_x, left)),
            copy(1, mine.at[:, lasts], beside.at[:, lasts], (my_x, right)),
            copy(2, edges.at[layer, 0], hrow.at[layer, 1], (up, my_y)),
            copy(3, edges.at[layer, 1], hrow.at[layer, 0], (down, my_y)),
            copy(4, mine.at[head, firsts], below.at[:, firsts], (up, left)),
            copy(5, mine.at[tail, firsts], above.at[:, firsts], (down, left)),
            copy(6, mine.at[head, lasts], below.at[:, lasts], (up, right)),
            copy(7, mine.at[tail, lasts], above.at[:, lasts], (down, right)),
        ]

    def a2a_copy(layer, k):
        target = (me + k) % devices
        return pltpu.make_async_remote_copy(
            src_ref=sendbuf.at[layer, pl.ds(target // sharers * slot, slot)],
            dst_ref=recv.at[layer, k - 1],
            send_sem=a2a_send.at[layer, k - 1],
            recv_sem=a2a_recv.at[layer, k - 1],
            device_id=place(target),
            device_id_type=MESH,
        )

    def gather_copy(layer, k):
        return pltpu.make_async_remote_copy(
            src_ref=mixed.at[layer],
            dst_ref=gath.at[layer, pl.ds(me * slot, slot)],
            send_sem=gat_send.at[layer, k - 1],
            recv_sem=gat_recv.at[layer, k - 1],
            device_id=place((me + k) % devices),
            device_id_type=MESH,
        )

    def turned(value):
        return jnp.where(
            (iota(value.shape, 1) // MODES_Y) % 2 == 1,
            pltpu.roll(value, MODES_Y, 1),
            -pltpu.roll(value, LANES - MODES_Y, 1),
        )

    def triple(value):
        high, low = split_bf16(value)
        return jnp.concatenate([high, low, high], axis=0)

    def row_transform(layer):
        @pl.loop(0, channels // batch, unroll=5 if channels // batch % 5 == 0 else 1)
        def _(b):
            parts = [
                triple(lines[pl.ds(b * batch + i, local_rows, stride=channels), :])
                for i in range(batch)
            ]
            result = jnp.dot(
                ftab[...], jnp.concatenate(parts, axis=1), preferred_element_type=f32
            )
            for i in range(batch):
                both = result[:, i * LANES : (i + 1) * LANES]
                total = both[:modes_x] + pltpu.roll(both[modes_x:], per_device, 1)
                block = total
                if share_rows == 2:
                    block = jnp.where(
                        iota((blocks, LANES), 1) < per_device,
                        total[:blocks],
                        pltpu.roll(total[blocks:], per_device, 1),
                    )
                sendbuf[layer, pl.ds(b * batch + i, blocks, stride=slot), :] = block

    def mix_modes(layer):
        own = sendbuf[layer, pl.ds(pl.multiple_of(me // sharers * slot, 8), slot), :]

        @pl.loop(1, devices)
        def _(k):
            a2a_copy(layer, k).wait_recv()

        own = own + jnp.sum(recv[layer], axis=0)
        crossed = turned(own)
        is_real = iota((2 * channels, LANES), 0) % 2 == 0

        def spread_lanes(part):
            if share_rows == 1:
                tiled = jnp.concatenate([part] * (LANES // share), axis=1)
                at = iota(tiled.shape, 1) // share
                return jnp.where(at % sharers == me % sharers, tiled, 0.0)
            pieces = []
            for j in range(share_rows):
                piece = part[:, j * MODES_Y : (j + 1) * MODES_Y]
                pieces += [piece, piece]
            return jnp.concatenate(pieces, axis=1)

        total = jnp.zeros((2 * channels, LANES), f32)
        for c in range(channels):
            weights = spread_lanes(sw_ref[layer, c].reshape(2 * channels, share))
            total = total + weights * jnp.where(is_real, own[c : c + 1], crossed[c : c + 1])
        pairs[...] = total
        total = pairs[pl.ds(0, channels, stride=2), :] + pairs[pl.ds(1, channels, stride=2), :]
        total = total * mixb[3 * layer : 3 * layer + 1, :LANES]
        mixed[layer, :channels, :] = total
        gath[layer, pl.ds(pl.multiple_of(me * slot, 8), channels), :] = total

        @pl.loop(1, devices)
        def _(k):
            gather_copy(layer, k).start()

    def inverse_rows(layer):
        @pl.loop(1, devices)
        def _(k):
            gather_copy(layer, k).wait_recv()

        @pl.loop(0, channels // batch, unroll=5 if channels // batch % 5 == 0 else 1)
        def _(b):
            parts = []
            for i in range(batch):
                o = b * batch + i
                block = gath[layer, pl.ds(o, blocks, stride=slot * sharers), :]
                for j in range(1, sharers):
                    block = block + gath[layer, pl.ds(j * slot + o, blocks, stride=slot * sharers), :]
                cross = turned(block)
                stack = [block, cross]
                if share_rows == 2:
                    stack = [block, pltpu.roll(block, per_device, 1)]
                    stack += [cross, pltpu.roll(cross, per_device, 1)]
                parts.append(triple(jnp.concatenate(stack, axis=0)))
            result = jnp.dot(
                itab[...], jnp.concatenate(parts, axis=1), preferred_element_type=f32
            )
            for i in range(batch):
                lhs[pl.ds(b * batch + i, local_rows, stride=channels), :] = result[
                    :, i * LANES : (i + 1) * LANES
                ]

    def conv_groups(layer, g, count):
        def window(rows, shifts, beside):
            own = [rows[:, s * LANES : (s + 1) * LANES] for s in range(planes)]
            at = iota((rows.shape[0], LANES), 1)
            known = {}

            def piece(s, d):
                q = s + d
                plane, move = q % planes, q // planes
                if (plane, move) not in known:
                    value = own[plane]
                    if move > 0:
                        value = jnp.where(at < move, beside(plane), value)
                    if move < 0:
                        value = jnp.where(at >= LANES + move, beside(plane), value)
                    if move:
                        value = pltpu.roll(value, (-move) % LANES, 1)
                    known[plane, move] = value
                return known[plane, move]

            return [jnp.concatenate([piece(s, d) for s in range(planes)], axis=1) for d in shifts]

        rows = nst[pl.ds(pl.multiple_of(g * whole, whole), (2 * count - 1) * half + depth), :]
        near_columns = window(rows, NEAR, lambda plane: rows[:, cols:])
        far_columns = []
        for p in range(2):
            rows = fst[p, pl.ds(pl.multiple_of(g * half, half), (count - 1) * half + depth), :]
            far_columns.append(
                window(rows, FAR, lambda s: rows[:, cols + s * LANES : cols + (s + 1) * LANES])
            )
        bias = jnp.concatenate([biasb[layer]] * planes, axis=1)

        def apply(weights, parts, start):
            columns = jnp.concatenate([part[start : start + depth] for part in parts], axis=0)
            return jnp.dot(weights, columns, preferred_element_type=f32)

        for i in range(count):
            near = [apply(nw[layer], near_columns, (2 * i + h) * half) for h in range(2)]
            parts = []
            for p in range(2):
                far = apply(fw[layer], far_columns[p], i * half)
                side = slice(p * 2 * pair, (p + 1) * 2 * pair)
                close = jnp.concatenate([near[0][side], near[1][side]], axis=0)
                total = (
                    mixb[3 * layer + 1 : 3 * layer + 2, :] * close
                    + mixb[3 * layer + 2 : 3 * layer + 3, :] * far
                    + bias
                )
                parts.append(total)
            conv[pl.ds(pl.multiple_of((g + i) * whole, whole), whole), :] = jnp.concatenate(
                parts, axis=0
            )

    def out_copy(g):
        rows = pl.ds(pl.multiple_of(g * whole, whole), whole)
        return pltpu.make_async_copy(obuf.at[rows], out_ref.at[rows], out_sem.at[g])

    def finish_pair(layer, b):
        spots = [pl.ds(pl.multiple_of((2 * b + i) * whole, whole), whole) for i in range(2)]
        values = []
        for at in spots:
            high, low = split_bf16(lhs[at, :per_device])
            spectral = jnp.dot(
                jnp.concatenate([high, low, high], axis=1), inv[...], preferred_element_type=f32
            )
            value = conv[at, :] + spectral
            value = value * 0.5 * (1.0 + lax.erf(value * (0.5**0.5)))
            values.append(value.astype(bf16))
        if layer + 1 < layers:
            ingest(2 * b, values)
        else:
            values = [
                jnp.dot(back[...], value, preferred_element_type=f32).astype(bf16)
                for value in values
            ]
            for i in range(2):
                obuf[spots[i], :] = values[i]
            for i in range(2):
                out_copy(2 * b + i).start()

    for layer in range(layers):
        packs[layer] = pack[...].astype(bf16)
        tops = [fst[p, : 2 * pair, :cols].astype(f32)[pair:] for p in range(2)]
        edges[layer, 0] = jnp.concatenate(tops, axis=0).astype(bf16)
        bottoms = [carry[p, :, :cols] for p in range(2)]
        edges[layer, 1] = jnp.concatenate(bottoms, axis=0).astype(bf16)
        halos = halo_copies(layer)
        for copy in halos:
            copy.start()
        row_transform(layer)

        @pl.loop(1, devices)
        def _(k):
            a2a_copy(layer, k).start()

        if layer == 0:
            spread_taps()
        for copy in halos[:2]:
            copy.wait_recv()
        carry[:, :, cols:] = jnp.zeros((2, pair, cols), f32)
        pack[...] = hcol[layer].astype(f32)

        @pl.loop(0, groups // 4)
        def _(b):
            parts = [edge_columns(pack[...], 8 * b + i) for i in range(8)]
            store_groups(4 * b, [(parts[2 * i], parts[2 * i + 1]) for i in range(4)], 1)

        twos = (groups - 2) // 2
        cut = first_part * twos // 14

        @pl.loop(0, cut)
        def _(b):
            conv_groups(layer, 1 + 2 * b, 2)

        mix_modes(layer)

        @pl.loop(cut, twos)
        def _(b):
            conv_groups(layer, 1 + 2 * b, 2)

        for copy in halos[2:]:
            copy.wait_recv()

        def halo_rows(side):
            k = 0 if side else 2 * (groups - 1)
            main = hrow[layer, side].astype(f32)
            out = []
            for p in range(2):
                corner = edge_columns(hcorner[layer, side].astype(f32), k + p)
                corner = corner[:pair] if side else corner[trim - pair :]
                out.append((main[p * pair : (p + 1) * pair], corner))
            return out

        above, below = halo_rows(0), halo_rows(1)
        first = slice(0, 2 * pair)

        def patch(rows, halo):
            return jnp.concatenate([halo, rows.astype(f32)[pair:]], axis=0).astype(bf16)

        nst[first, :cols] = patch(nst[first, :cols], above[1][0])
        nst[first, cols:] = patch(nst[first, cols:], near_edges(above[1][1]))
        end = groups * whole
        last = slice(end, end + 2 * pair)
        nst[last, :cols] = jnp.concatenate([carry[1, :, :cols], below[0][0]], axis=0).astype(bf16)
        nst[last, cols:] = near_edges(
            jnp.concatenate([carry[1, :, cols:], below[0][1]], axis=0)
        ).astype(bf16)
        end = groups * half
        last = slice(end, end + 2 * pair)
        for p in range(2):
            for side in range(2):
                at = slice(side * cols, (side + 1) * cols)
                fst[p, first, at] = patch(fst[p, first, at], above[p][side])
                fst[p, last, at] = jnp.concatenate(
                    [carry[p, :, at], below[p][side]], axis=0
                ).astype(bf16)

        @pl.loop(0, 2)
        def _(i):
            conv_groups(layer, i * (groups - 1), 1)

        inverse_rows(layer)
        carry[...] = jnp.zeros_like(carry)
        pack[...] = jnp.zeros_like(pack)

        @pl.loop(0, groups // 2)
        def _(b):
            finish_pair(layer, b)

        for copy in halos:
            copy.wait_send()

        @pl.loop(1, devices)
        def _(k):
            a2a_copy(layer, k).wait_send()
            gather_copy(layer, k).wait_send()

    @pl.loop(0, groups)
    def _(g):
        out_copy(g).wait()


def main_call(u, weights, near, far, rtab, ctab, mix, bias, sizes, cells):
    channels, local_rows, cols = u.shape
    layers = weights.shape[0]
    devices = sizes[0] * sizes[1]
    pair = 2 * channels
    half = 4 * pair
    slot = (channels + 7) // 8 * 8
    blocks = devices * min(weights.shape[-1], MODES_Y) // MODES_Y
    groups = local_rows // GROUP
    modes_x = rtab.shape[0] // 2
    depth = 6 * pair
    wide = (depth + LANES - 1) // LANES * LANES
    trim = (pair + 15) // 16 * 16
    vmem = pl.BlockSpec(memory_space=pltpu.VMEM)
    anywhere = pl.BlockSpec(memory_space=pl.ANY)
    dma = pltpu.SemaphoreType.DMA
    scratch = pltpu.VMEM
    return pl.pallas_call(
        functools.partial(
            main_kernel, sizes=sizes, cells=cells, first_part=6,
            batch=4 if channels % 4 == 0 else 1,
        ),
        name="operator",
        out_shape=jax.ShapeDtypeStruct((groups * 2 * half, cols), bf16),
        in_specs=[anywhere] + [vmem] * 7,
        out_specs=anywhere,
        scratch_shapes=[
            scratch((channels, local_rows, cols), bf16),
            scratch((groups * 2 * half, cols), bf16),
            scratch((groups * 2 * half + 2 * pair, cols + LANES), bf16),
            scratch((2, groups * half + 2 * pair, 2 * cols), bf16),
            scratch((groups * 2 * half, cols), f32),
            scratch((groups * 2 * half, LANES), f32),
            scratch((groups * 2 * half, LANES), f32),
            scratch((2, pair, 2 * cols), f32),
            scratch((half, 2 * LANES), f32),
            scratch((layers, half, 2 * LANES), bf16),
            scratch((layers, 2, 2 * pair, cols), bf16),
            scratch((layers, half, 2 * LANES), bf16),
            scratch((layers, 2, 2 * pair, cols), bf16),
            scratch((layers, 2, trim, 2 * LANES), bf16),
            scratch((layers, blocks * slot, LANES), f32),
            scratch((layers, devices - 1, slot, LANES), f32),
            scratch((layers, slot, LANES), f32),
            scratch((layers, devices * slot, LANES), f32),
            scratch((layers, half, 3 * depth), bf16),
            scratch((layers, half, 5 * depth), bf16),
            scratch((layers * channels, 4 * LANES), f32),
            scratch((8 * layers * channels, wide), f32),
            scratch((2 * modes_x, 3 * local_rows), bf16),
            scratch((local_rows, 6 * modes_x), bf16),
            scratch((cols, LANES), bf16),
            scratch((6 * MODES_Y, cols), bf16),
            scratch((8, cols), f32),
            scratch((layers, half, LANES), f32),
            scratch((2 * LANES, cols), jnp.int32),
            scratch((2 * channels, LANES), f32),
            scratch((2 * half, 2 * half), bf16),
            scratch((2 * half, 2 * half), bf16),
            scratch((cols, cols), bf16),
            scratch((layers * half, 8 * layers * channels), bf16),
            scratch((2 * LANES, cols), bf16),
            dma((groups,)),
            dma((groups,)),
            dma((layers, 8)),
            dma((layers, 8)),
            dma((layers, devices - 1)),
            dma((layers, devices - 1)),
            dma((layers, devices - 1)),
            dma((layers, devices - 1)),
        ],
        compiler_params=pltpu.CompilerParams(
            collective_id=0, has_side_effects=True, vmem_limit_bytes=62 * 1024 * 1024
        ),
    )(u, weights, near, far, rtab, ctab, mix, bias)


def solution(mesh):
    sizes = (mesh.shape["gx"], mesh.shape["gy"])

    def on_device(grid_field, spectral_weight, conv_near, conv_far, mix_logits, channel_bias):
        _, channels, local_rows, local_cols = grid_field.shape
        layers = spectral_weight.shape[0]
        share = spectral_weight.shape[-1]
        devices = sizes[0] * sizes[1]
        cells_x, cells_y = local_rows * sizes[0], local_cols * sizes[1]
        modes_x = share * devices // MODES_Y
        per_share = max(share // MODES_Y, 1)
        blocks = modes_x // per_share
        groups = local_rows // GROUP
        planes = local_cols // LANES
        assert share * per_share in (16, 32, 128)
        assert groups * GROUP == local_rows and 8 * groups <= LANES and groups >= 4
        assert groups % 4 == 0
        assert cells_x % 4 == 0 and cells_y % 4 == 0
        assert planes * LANES == local_cols and planes in (1, 2, 4)

        mode = jnp.arange(2 * modes_x, dtype=jnp.int32)
        slot = mode % modes_x % blocks * per_share + mode % modes_x // blocks
        row_mode = jnp.where(slot < modes_x // 2, slot, slot + (cells_x - modes_x))
        turn = jnp.where(mode < modes_x, 0, 3 * cells_x // 4)
        index = jnp.arange(local_rows, dtype=jnp.int32)
        row_at = index // GROUP * GROUP + group_order(index % GROUP)
        row_at = row_at + lax.axis_index("gx") * local_rows
        phase = (row_mode[:, None] * row_at[None, :] + turn[:, None]) % cells_x
        rtab = jnp.cos(phase.astype(f32) * (full_turn / cells_x))

        index = jnp.arange(local_cols, dtype=jnp.int32)
        col_at = lax.axis_index("gy") * local_cols + natural_column(index, local_cols)
        mode = jnp.arange(2 * MODES_Y, dtype=jnp.int32)
        turn = jnp.where(mode < MODES_Y, 0, cells_y // 4)
        phase = ((mode % MODES_Y)[:, None] * col_at[None, :] + turn[:, None]) % cells_y
        ctab = jnp.cos(phase.astype(f32) * (full_turn / cells_y))

        field = main_call(
            grid_field[0],
            spectral_weight.transpose(0, 2, 3, 1, 4),
            conv_near.transpose(1, 0, 2),
            conv_far.transpose(1, 0, 2),
            rtab, ctab, mix_logits, channel_bias,
            sizes, cells_x * cells_y,
        )
        return restore_call(field, channels)[None]

    in_specs = (
        P(None, None, "gx", "gy"),
        P(None, None, None, None, ("gx", "gy")),
        P(),
        P(),
        P(),
        P(),
    )
    return jax.shard_map(
        on_device,
        mesh=mesh,
        in_specs=in_specs,
        out_specs=P(None, None, "gx", "gy"),
        check_vma=False,
    )
```

```python
import functools
import math

import jax
import jax.numpy as jnp
from jax import lax
from jax.experimental import pallas as pl
from jax.experimental.pallas import tpu as pltpu
from jax.sharding import PartitionSpec as P

full_turn = 2.0 * math.pi
MESH = pl.DeviceIdType.MESH
MODES_Y = 32
GROUP = 16
LANES = 128
HALO = 4
CHUNK = 4
NEAR = (-1, 0, 1)
FAR = (-4, -2, 0, 2, 4)
f32 = jnp.float32
bf16 = jnp.bfloat16


def split_bf16(value):
    high = value.astype(bf16)
    low = (value - high.astype(f32)).astype(bf16)
    return high, low


def group_order(place):
    return place % 8 // 2 * 4 + place % 2 * 2 + place // 8


def iota(shape, dim):
    return lax.broadcasted_iota(jnp.int32, shape, dim)


def natural_order(at, channels):
    return at % channels * GROUP + group_order(at // channels)


def natural_column(at, cols):
    return at % LANES * (cols // LANES) + at // LANES


def matches(left, right):
    return jnp.where(left == right, 1.0, 0.0).astype(bf16)


def restore_kernel(value_ref, out_ref, columns, *, chunk):
    channels, _, cols = out_ref.shape
    whole = channels * GROUP

    @pl.when(pl.program_id(0) == 0)
    def _():
        at = natural_column(iota((cols, LANES), 0), cols)[:, :1]
        columns[...] = matches(at, iota((cols, cols), 1))

    for i in range(chunk):
        value = value_ref[i * whole : (i + 1) * whole, :]
        value = jnp.dot(value, columns[...], preferred_element_type=f32).astype(bf16)
        out_ref[:, i * GROUP : (i + 1) * GROUP, :] = value.reshape(channels, GROUP, cols)


def restore_call(value, channels):
    whole = channels * GROUP
    groups, cols = value.shape[0] // whole, value.shape[1]
    chunk = CHUNK if groups % CHUNK == 0 else 1
    return pl.pallas_call(
        functools.partial(restore_kernel, chunk=chunk),
        grid=(groups // chunk,),
        name="restore",
        in_specs=[pl.BlockSpec((chunk * whole, cols), lambda i: (i, 0))],
        out_specs=pl.BlockSpec((channels, chunk * GROUP, cols), lambda i: (0, i, 0)),
        out_shape=jax.ShapeDtypeStruct((channels, groups * GROUP, cols), bf16),
        scratch_shapes=[pltpu.VMEM((cols, cols), bf16)],
    )(value)


def main_kernel(
    u_ref, sw_ref, near_ref, far_ref, rtab_ref, ctab_ref,
    mix_ref, bias_ref, out_ref,
    ubuf, obuf, nst, fst, conv, lhs, lines, carry, pack, packs, edges, hcol, hrow, hcorner,
    sendbuf, recv, mixed, gath, nw, fw, taps, tall, ftab, itab, fwd, inv, mixb, biasb, code, pairs,
    order, back, columns, stack, pick,
    u_sem, out_sem, halo_send, halo_recv, a2a_send, a2a_recv, gat_send, gat_recv,
    *, sizes, cells, first_part, batch,
):
    gx, gy = sizes
    devices = gx * gy
    layers = sw_ref.shape[0]
    channels, local_rows, cols = ubuf.shape
    pair = 2 * channels
    half = 4 * pair
    whole = 2 * half
    groups = local_rows // GROUP
    planes = cols // LANES
    edge = HALO // planes
    slot = mixed.shape[1]
    blocks = sendbuf.shape[1] // slot
    sharers = devices // blocks
    per_device = 2 * MODES_Y
    modes_x = rtab_ref.shape[0] // 2
    share_rows = modes_x // blocks
    share = sw_ref.shape[-1]
    trim = (pair + 15) // 16 * 16
    my_x, my_y = lax.axis_index("gx"), lax.axis_index("gy")
    me = my_x * gy + my_y

    def place(index):
        return (index // gy, index % gy)

    barrier = pltpu.get_barrier_semaphore()

    def u_copy(g):
        rows = pl.ds(pl.multiple_of(g * GROUP, GROUP), GROUP)
        return pltpu.make_async_copy(u_ref.at[:, rows, :], ubuf.at[:, rows, :], u_sem.at[g])

    @pl.loop(0, groups)
    def _(g):
        u_copy(g).start()

    @pl.loop(1, devices)
    def _(k):
        pl.semaphore_signal(
            barrier, inc=1, device_id=place((me + k) % devices), device_id_type=MESH
        )

    at = natural_order(iota((whole, LANES), 0), channels)[:, :1]
    order[...] = matches(at, iota((whole, whole), 1))
    at = natural_order(iota((8, whole), 1), channels)[:1]
    back[...] = matches(iota((whole, whole), 0), at)
    at = natural_column(iota((8, cols), 1), cols)[:1]
    columns[...] = matches(iota((cols, cols), 0), at)
    at = iota((layers * half, LANES), 0)
    wanted = at % half // channels * (layers * channels) + at % channels * layers + at // half
    stack[...] = matches(wanted[:, :1], iota(stack.shape, 1))

    high, low = split_bf16(rtab_ref[...])
    ftab[...] = jnp.concatenate([high, high, low], axis=1)
    high, low = split_bf16(rtab_ref[...].T)
    itab[...] = jnp.concatenate([high, high, low], axis=1)
    turned_cols = ctab_ref[...]
    cosine, sine = turned_cols[:MODES_Y], turned_cols[MODES_Y:]
    fwd[...] = jnp.concatenate([cosine, sine, sine, -cosine], axis=0).T.astype(bf16)
    weight = jnp.where(iota((per_device, cols), 0) % MODES_Y == 0, 1.0, 2.0) / cells
    high, low = split_bf16(turned_cols * weight)
    inv[...] = jnp.concatenate([high, high, low], axis=0)

    exponents = jnp.exp(mix_ref[...])
    mixtures = exponents / jnp.sum(exponents, axis=1, keepdims=True)
    for layer in range(layers):
        for i in range(3):
            at = 3 * layer + i
            mixb[at : at + 1, :] = jnp.broadcast_to(
                mixtures[layer : layer + 1, i : i + 1], (1, cols)
            )
        same = iota((half, channels), 0) % channels == iota((half, channels), 1)
        column = jnp.sum(
            jnp.where(same, bias_ref[layer : layer + 1, :], 0.0), axis=1, keepdims=True
        )
        biasb[layer] = jnp.broadcast_to(column, (half, LANES))

    at, lane_at = iota(code.shape, 0), iota(code.shape, 1)
    plane, lane = lane_at // LANES, lane_at % LANES
    before = planes * (lane - (LANES - edge)) + plane
    after = planes * lane + plane
    code[...] = jnp.where(
        (at < LANES) & (lane >= LANES - edge),
        at - before,
        jnp.where((at >= LANES) & (lane < edge), at - LANES - after, -1),
    )

    pick[...] = matches(code[...], 0)

    def roll_halves(value, amount):
        return jnp.concatenate(
            [pltpu.roll(value[:, i * LANES : (i + 1) * LANES], amount, 1) for i in range(2)], axis=1
        )

    def edge_columns(packed, k):
        turned_back = roll_halves(packed, (LANES - HALO * k) % LANES).astype(bf16)
        return jnp.dot(turned_back, pick[...], preferred_element_type=f32)

    depth = 6 * pair
    wide = (depth + LANES - 1) // LANES * LANES

    def tap_rows(taps_ref):
        count = taps_ref.shape[2]
        for o in range(channels):
            taps[layers * o : layers * (o + 1), :count] = taps_ref[o].astype(f32)
        return taps[:, :count].astype(bf16)

    rows_of = layers * channels

    def spread(out_ref, index):
        stacked = tall[...].astype(bf16)
        full = jnp.dot(stack[...], stacked, preferred_element_type=f32).astype(bf16)
        return [full[layer * half : (layer + 1) * half, :depth] for layer in range(layers)]

    def emit(out_ref, pieces):
        for layer in range(layers):
            out_ref[layer] = jnp.concatenate([piece[layer] for piece in pieces], axis=1)

    def spread_taps():
        source = tap_rows(far_ref)
        count = far_ref.shape[2]
        target = iota((count, wide), 1)
        base = jnp.where(
            target < 5 * channels,
            target // channels * (5 * channels) + target % channels,
            -count,
        )
        base = iota((count, wide), 0) - base
        pieces = []
        for column in range(5):
            chosen = matches(base, column * channels)
            block = jnp.dot(source, chosen, preferred_element_type=f32)
            for row in range(8):
                tall[rows_of * row : rows_of * (row + 1), :] = (
                    pltpu.roll(block, channels * row, 1) if row else block
                )
            pieces.append(spread(fw, column))
        emit(fw, pieces)

        source = tap_rows(near_ref)
        count = near_ref.shape[2]
        target = iota((count, wide), 1)
        spot, channel = target // channels, target % channels
        where_row = {-1: 1, 0: 2, 1: 4, 2: 3, 3: 5, 4: 6}
        bases = []
        for row in range(4):
            tap = jnp.full(target.shape, -count, jnp.int32)
            for step in range(3):
                tap = jnp.where(
                    spot == where_row[row + step - 1], step * 3 * channels + channel, tap
                )
            bases.append(iota((count, wide), 0) - tap)
        pieces = []
        for column in range(3):
            for row in range(4):
                chosen = matches(bases[row], column * channels)
                block = jnp.dot(source, chosen, preferred_element_type=f32)
                for quad in range(2):
                    full_row = 4 * quad + row
                    index = full_row % 2 * 4 + full_row // 2
                    tall[rows_of * index : rows_of * (index + 1), :] = (
                        pltpu.roll(block, 4 * channels, 1) if quad else block
                    )
            pieces.append(spread(nw, column))
        emit(nw, pieces)

    def near_edges(value):
        low_lanes = iota((value.shape[0], LANES), 1) < LANES // 2
        return jnp.where(low_lanes, value[:, :LANES], value[:, cols - LANES :])

    def store_groups(first, values, side):
        at = slice(side * cols, (side + 1) * cols)
        old = carry[0, :, at], carry[1, :, at]
        for i, (even, odd) in enumerate(values):
            old = store_rows(first + i, even, odd, old, side)
        carry[0, :, at], carry[1, :, at] = old

    def store_rows(g, even, odd, old, side):
        at = slice(side * cols, (side + 1) * cols)
        old_even, old_odd = old
        q = [(even[i * pair : (i + 1) * pair], odd[i * pair : (i + 1) * pair]) for i in range(4)]
        near_rows = [old_odd]
        for i in range(4):
            near_rows.append(q[i][0])
            if i < 3:
                near_rows.append(q[i][1])
        near_rows = jnp.concatenate(near_rows, axis=0)
        near_at = pl.ds(pl.multiple_of(g * whole, whole), whole)
        if side:
            nst[near_at, cols:] = near_edges(near_rows).astype(bf16)
        else:
            nst[near_at, :cols] = near_rows.astype(bf16)
        row = pl.ds(pl.multiple_of(g * half, half), half)
        fst[0, row, at] = jnp.concatenate([old_even, even[: 3 * pair]], axis=0).astype(bf16)
        fst[1, row, at] = jnp.concatenate([old_odd, odd[: 3 * pair]], axis=0).astype(bf16)
        return q[3]

    def ingest(first, values):
        total = pack[...]
        sums, parts = [], []
        for i, value in enumerate(values):
            sums.append(jnp.dot(value, fwd[...], preferred_element_type=f32))
            for p in range(2):
                found = lax.dot_general(
                    value[p * half : (p + 1) * half],
                    pick[...],
                    (((1,), (1,)), ((), ())),
                    preferred_element_type=f32,
                )
                total = total + roll_halves(found, HALO * (2 * (first + i) + p))
            full = value.astype(f32)
            parts.append((full[:half], full[half:]))
        pack[...] = total
        for i, found in enumerate(sums):
            lines[pl.ds(pl.multiple_of((first + i) * whole, whole), whole), :] = found
        store_groups(first, parts, 0)

    carry[...] = jnp.zeros_like(carry)
    pack[...] = jnp.zeros_like(pack)

    @pl.loop(0, groups // 4)
    def _(b):
        values = []
        for i in range(4):
            u_copy(4 * b + i).wait()
        for i in range(4):
            at = pl.ds(pl.multiple_of((4 * b + i) * GROUP, GROUP), GROUP)
            slab = ubuf[:, at, :].reshape(whole, cols)
            values.append(jnp.dot(order[...], slab, preferred_element_type=f32).astype(bf16))
        values = [
            jnp.dot(value, columns[...], preferred_element_type=f32).astype(bf16)
            for value in values
        ]
        ingest(4 * b, values)

    pl.semaphore_wait(barrier, devices - 1)

    up, down = (my_x + gx - 1) % gx, (my_x + 1) % gx
    left, right = (my_y + gy - 1) % gy, (my_y + 1) % gy

    def halo_copies(layer):
        def copy(i, src, dst, target):
            return pltpu.make_async_remote_copy(
                src_ref=src, dst_ref=dst, send_sem=halo_send.at[layer, i],
                recv_sem=halo_recv.at[layer, i], device_id=target, device_id_type=MESH,
            )

        mine, beside = packs.at[layer], hcol.at[layer]
        above, below = hcorner.at[layer, 0], hcorner.at[layer, 1]
        lasts, firsts = slice(0, LANES), slice(LANES, 2 * LANES)
        head, tail = slice(0, trim), slice(half - trim, half)
        return [
            copy(0, mine.at[:, firsts], beside.at[:, firsts], (my_x, left)),
            copy(1, mine.at[:, lasts], beside.at[:, lasts], (my_x, right)),
            copy(2, edges.at[layer, 0], hrow.at[layer, 1], (up, my_y)),
            copy(3, edges.at[layer, 1], hrow.at[layer, 0], (down, my_y)),
            copy(4, mine.at[head, firsts], below.at[:, firsts], (up, left)),
            copy(5, mine.at[tail, firsts], above.at[:, firsts], (down, left)),
            copy(6, mine.at[head, lasts], below.at[:, lasts], (up, right)),
            copy(7, mine.at[tail, lasts], above.at[:, lasts], (down, right)),
        ]

    def a2a_copy(layer, k):
        target = (me + k) % devices
        return pltpu.make_async_remote_copy(
            src_ref=sendbuf.at[layer, pl.ds(target // sharers * slot, slot)],
            dst_ref=recv.at[layer, k - 1],
            send_sem=a2a_send.at[layer, k - 1],
            recv_sem=a2a_recv.at[layer, k - 1],
            device_id=place(target),
            device_id_type=MESH,
        )

    def gather_copy(layer, k):
        return pltpu.make_async_remote_copy(
            src_ref=mixed.at[layer],
            dst_ref=gath.at[layer, pl.ds(me * slot, slot)],
            send_sem=gat_send.at[layer, k - 1],
            recv_sem=gat_recv.at[layer, k - 1],
            device_id=place((me + k) % devices),
            device_id_type=MESH,
        )

    def turned(value):
        return jnp.where(
            (iota(value.shape, 1) // MODES_Y) % 2 == 1,
            pltpu.roll(value, MODES_Y, 1),
            -pltpu.roll(value, LANES - MODES_Y, 1),
        )

    def triple(value):
        high, low = split_bf16(value)
        return jnp.concatenate([high, low, high], axis=0)

    def row_transform(layer):
        @pl.loop(0, channels // batch, unroll=5 if channels // batch % 5 == 0 else 1)
        def _(b):
            parts = [
                triple(lines[pl.ds(b * batch + i, local_rows, stride=channels), :])
                for i in range(batch)
            ]
            result = jnp.dot(
                ftab[...], jnp.concatenate(parts, axis=1), preferred_element_type=f32
            )
            for i in range(batch):
                both = result[:, i * LANES : (i + 1) * LANES]
                total = both[:modes_x] + pltpu.roll(both[modes_x:], per_device, 1)
                block = total
                if share_rows == 2:
                    block = jnp.where(
                        iota((blocks, LANES), 1) < per_device,
                        total[:blocks],
                        pltpu.roll(total[blocks:], per_device, 1),
                    )
                sendbuf[layer, pl.ds(b * batch + i, blocks, stride=slot), :] = block

    def mix_modes(layer):
        own = sendbuf[layer, pl.ds(pl.multiple_of(me // sharers * slot, 8), slot), :]

        @pl.loop(1, devices)
        def _(k):
            a2a_copy(layer, k).wait_recv()

        own = own + jnp.sum(recv[layer], axis=0)
        crossed = turned(own)
        is_real = iota((2 * channels, LANES), 0) % 2 == 0

        def spread_lanes(part):
            if share_rows == 1:
                tiled = jnp.concatenate([part] * (LANES // share), axis=1)
                at = iota(tiled.shape, 1) // share
                return jnp.where(at % sharers == me % sharers, tiled, 0.0)
            pieces = []
            for j in range(share_rows):
                piece = part[:, j * MODES_Y : (j + 1) * MODES_Y]
                pieces += [piece, piece]
            return jnp.concatenate(pieces, axis=1)

        total = jnp.zeros((2 * channels, LANES), f32)
        for c in range(channels):
            weights = spread_lanes(sw_ref[layer, c].reshape(2 * channels, share))
            total = total + weights * jnp.where(is_real, own[c : c + 1], crossed[c : c + 1])
        pairs[...] = total
        total = pairs[pl.ds(0, channels, stride=2), :] + pairs[pl.ds(1, channels, stride=2), :]
        total = total * mixb[3 * layer : 3 * layer + 1, :LANES]
        mixed[layer, :channels, :] = total
        gath[layer, pl.ds(pl.multiple_of(me * slot, 8), channels), :] = total

        @pl.loop(1, devices)
        def _(k):
            gather_copy(layer, k).start()

    def inverse_rows(layer):
        @pl.loop(1, devices)
        def _(k):
            gather_copy(layer, k).wait_recv()

        @pl.loop(0, channels // batch, unroll=5 if channels // batch % 5 == 0 else 1)
        def _(b):
            parts = []
            for i in range(batch):
                o = b * batch + i
                block = gath[layer, pl.ds(o, blocks, stride=slot * sharers), :]
                for j in range(1, sharers):
                    block = block + gath[layer, pl.ds(j * slot + o, blocks, stride=slot * sharers), :]
                cross = turned(block)
                stack = [block, cross]
                if share_rows == 2:
                    stack = [block, pltpu.roll(block, per_device, 1)]
                    stack += [cross, pltpu.roll(cross, per_device, 1)]
                parts.append(triple(jnp.concatenate(stack, axis=0)))
            result = jnp.dot(
                itab[...], jnp.concatenate(parts, axis=1), preferred_element_type=f32
            )
            for i in range(batch):
                lhs[pl.ds(b * batch + i, local_rows, stride=channels), :] = result[
                    :, i * LANES : (i + 1) * LANES
                ]

    def conv_groups(layer, g, count):
        def window(rows, shifts, beside):
            own = [rows[:, s * LANES : (s + 1) * LANES] for s in range(planes)]
            at = iota((rows.shape[0], LANES), 1)
            known = {}

            def piece(s, d):
                q = s + d
                plane, move = q % planes, q // planes
                if (plane, move) not in known:
                    value = own[plane]
                    if move > 0:
                        value = jnp.where(at < move, beside(plane), value)
                    if move < 0:
                        value = jnp.where(at >= LANES + move, beside(plane), value)
                    if move:
                        value = pltpu.roll(value, (-move) % LANES, 1)
                    known[plane, move] = value
                return known[plane, move]

            return [jnp.concatenate([piece(s, d) for s in range(planes)], axis=1) for d in shifts]

        rows = nst[pl.ds(pl.multiple_of(g * whole, whole), (2 * count - 1) * half + depth), :]
        near_columns = window(rows, NEAR, lambda plane: rows[:, cols:])
        far_columns = []
        for p in range(2):
            rows = fst[p, pl.ds(pl.multiple_of(g * half, half), (count - 1) * half + depth), :]
            far_columns.append(
                window(rows, FAR, lambda s: rows[:, cols + s * LANES : cols + (s + 1) * LANES])
            )
        bias = jnp.concatenate([biasb[layer]] * planes, axis=1)

        def apply(weights, parts, start):
            columns = jnp.concatenate([part[start : start + depth] for part in parts], axis=0)
            return jnp.dot(weights, columns, preferred_element_type=f32)

        for i in range(count):
            near = [apply(nw[layer], near_columns, (2 * i + h) * half) for h in range(2)]
            parts = []
            for p in range(2):
                far = apply(fw[layer], far_columns[p], i * half)
                side = slice(p * 2 * pair, (p + 1) * 2 * pair)
                close = jnp.concatenate([near[0][side], near[1][side]], axis=0)
                total = (
                    mixb[3 * layer + 1 : 3 * layer + 2, :] * close
                    + mixb[3 * layer + 2 : 3 * layer + 3, :] * far
                    + bias
                )
                parts.append(total)
            conv[pl.ds(pl.multiple_of((g + i) * whole, whole), whole), :] = jnp.concatenate(
                parts, axis=0
            )

    def out_copy(g):
        rows = pl.ds(pl.multiple_of(g * whole, whole), whole)
        return pltpu.make_async_copy(obuf.at[rows], out_ref.at[rows], out_sem.at[g])

    def finish_groups(layer, b):
        spots = [pl.ds(pl.multiple_of((4 * b + i) * whole, whole), whole) for i in range(4)]
        values = []
        for at in spots:
            high, low = split_bf16(lhs[at, :per_device])
            spectral = jnp.dot(
                jnp.concatenate([high, low, high], axis=1), inv[...], preferred_element_type=f32
            )
            value = conv[at, :] + spectral
            value = value * 0.5 * (1.0 + lax.erf(value * (0.5**0.5)))
            values.append(value.astype(bf16))
        if layer + 1 < layers:
            ingest(4 * b, values)
        else:
            values = [
                jnp.dot(back[...], value, preferred_element_type=f32).astype(bf16)
                for value in values
            ]
            for i in range(4):
                obuf[spots[i], :] = values[i]
            for i in range(4):
                out_copy(4 * b + i).start()

    for layer in range(layers):
        packs[layer] = pack[...].astype(bf16)
        tops = [fst[p, : 2 * pair, :cols].astype(f32)[pair:] for p in range(2)]
        edges[layer, 0] = jnp.concatenate(tops, axis=0).astype(bf16)
        bottoms = [carry[p, :, :cols] for p in range(2)]
        edges[layer, 1] = jnp.concatenate(bottoms, axis=0).astype(bf16)
        halos = halo_copies(layer)
        for copy in halos:
            copy.start()
        row_transform(layer)

        @pl.loop(1, devices)
        def _(k):
            a2a_copy(layer, k).start()

        if layer == 0:
            spread_taps()
        for copy in halos[:2]:
            copy.wait_recv()
        carry[:, :, cols:] = jnp.zeros((2, pair, cols), f32)
        pack[...] = hcol[layer].astype(f32)

        @pl.loop(0, groups // 4)
        def _(b):
            parts = [edge_columns(pack[...], 8 * b + i) for i in range(8)]
            store_groups(4 * b, [(parts[2 * i], parts[2 * i + 1]) for i in range(4)], 1)

        twos = (groups - 2) // 2
        cut = first_part * twos // 14

        @pl.loop(0, cut)
        def _(b):
            conv_groups(layer, 1 + 2 * b, 2)

        mix_modes(layer)

        @pl.loop(cut, twos)
        def _(b):
            conv_groups(layer, 1 + 2 * b, 2)

        for copy in halos[2:]:
            copy.wait_recv()

        def halo_rows(side):
            k = 0 if side else 2 * (groups - 1)
            main = hrow[layer, side].astype(f32)
            out = []
            for p in range(2):
                corner = edge_columns(hcorner[layer, side].astype(f32), k + p)
                corner = corner[:pair] if side else corner[trim - pair :]
                out.append((main[p * pair : (p + 1) * pair], corner))
            return out

        above, below = halo_rows(0), halo_rows(1)
        first = slice(0, 2 * pair)

        def patch(rows, halo):
            return jnp.concatenate([halo, rows.astype(f32)[pair:]], axis=0).astype(bf16)

        nst[first, :cols] = patch(nst[first, :cols], above[1][0])
        nst[first, cols:] = patch(nst[first, cols:], near_edges(above[1][1]))
        end = groups * whole
        last = slice(end, end + 2 * pair)
        nst[last, :cols] = jnp.concatenate([carry[1, :, :cols], below[0][0]], axis=0).astype(bf16)
        nst[last, cols:] = near_edges(
            jnp.concatenate([carry[1, :, cols:], below[0][1]], axis=0)
        ).astype(bf16)
        end = groups * half
        last = slice(end, end + 2 * pair)
        for p in range(2):
            for side in range(2):
                at = slice(side * cols, (side + 1) * cols)
                fst[p, first, at] = patch(fst[p, first, at], above[p][side])
                fst[p, last, at] = jnp.concatenate(
                    [carry[p, :, at], below[p][side]], axis=0
                ).astype(bf16)

        @pl.loop(0, 2)
        def _(i):
            conv_groups(layer, i * (groups - 1), 1)

        inverse_rows(layer)
        carry[...] = jnp.zeros_like(carry)
        pack[...] = jnp.zeros_like(pack)

        @pl.loop(0, groups // 4)
        def _(b):
            finish_groups(layer, b)

        for copy in halos:
            copy.wait_send()

        @pl.loop(1, devices)
        def _(k):
            a2a_copy(layer, k).wait_send()
            gather_copy(layer, k).wait_send()

    @pl.loop(0, groups)
    def _(g):
        out_copy(g).wait()


def main_call(u, weights, near, far, rtab, ctab, mix, bias, sizes, cells):
    channels, local_rows, cols = u.shape
    layers = weights.shape[0]
    devices = sizes[0] * sizes[1]
    pair = 2 * channels
    half = 4 * pair
    slot = (channels + 7) // 8 * 8
    blocks = devices * min(weights.shape[-1], MODES_Y) // MODES_Y
    groups = local_rows // GROUP
    modes_x = rtab.shape[0] // 2
    depth = 6 * pair
    wide = (depth + LANES - 1) // LANES * LANES
    trim = (pair + 15) // 16 * 16
    vmem = pl.BlockSpec(memory_space=pltpu.VMEM)
    anywhere = pl.BlockSpec(memory_space=pl.ANY)
    dma = pltpu.SemaphoreType.DMA
    scratch = pltpu.VMEM
    return pl.pallas_call(
        functools.partial(
            main_kernel, sizes=sizes, cells=cells, first_part=6,
            batch=4 if channels % 4 == 0 else 1,
        ),
        name="operator",
        out_shape=jax.ShapeDtypeStruct((groups * 2 * half, cols), bf16),
        in_specs=[anywhere] + [vmem] * 7,
        out_specs=anywhere,
        scratch_shapes=[
            scratch((channels, local_rows, cols), bf16),
            scratch((groups * 2 * half, cols), bf16),
            scratch((groups * 2 * half + 2 * pair, cols + LANES), bf16),
            scratch((2, groups * half + 2 * pair, 2 * cols), bf16),
            scratch((groups * 2 * half, cols), f32),
            scratch((groups * 2 * half, LANES), f32),
            scratch((groups * 2 * half, LANES), f32),
            scratch((2, pair, 2 * cols), f32),
            scratch((half, 2 * LANES), f32),
            scratch((layers, half, 2 * LANES), bf16),
            scratch((layers, 2, 2 * pair, cols), bf16),
            scratch((layers, half, 2 * LANES), bf16),
            scratch((layers, 2, 2 * pair, cols), bf16),
            scratch((layers, 2, trim, 2 * LANES), bf16),
            scratch((layers, blocks * slot, LANES), f32),
            scratch((layers, devices - 1, slot, LANES), f32),
            scratch((layers, slot, LANES), f32),
            scratch((layers, devices * slot, LANES), f32),
            scratch((layers, half, 3 * depth), bf16),
            scratch((layers, half, 5 * depth), bf16),
            scratch((layers * channels, 4 * LANES), f32),
            scratch((8 * layers * channels, wide), f32),
            scratch((2 * modes_x, 3 * local_rows), bf16),
            scratch((local_rows, 6 * modes_x), bf16),
            scratch((cols, LANES), bf16),
            scratch((6 * MODES_Y, cols), bf16),
            scratch((8, cols), f32),
            scratch((layers, half, LANES), f32),
            scratch((2 * LANES, cols), jnp.int32),
            scratch((2 * channels, LANES), f32),
            scratch((2 * half, 2 * half), bf16),
            scratch((2 * half, 2 * half), bf16),
            scratch((cols, cols), bf16),
            scratch((layers * half, 8 * layers * channels), bf16),
            scratch((2 * LANES, cols), bf16),
            dma((groups,)),
            dma((groups,)),
            dma((layers, 8)),
            dma((layers, 8)),
            dma((layers, devices - 1)),
            dma((layers, devices - 1)),
            dma((layers, devices - 1)),
            dma((layers, devices - 1)),
        ],
        compiler_params=pltpu.CompilerParams(
            collective_id=0, has_side_effects=True, vmem_limit_bytes=62 * 1024 * 1024
        ),
    )(u, weights, near, far, rtab, ctab, mix, bias)


def solution(mesh):
    sizes = (mesh.shape["gx"], mesh.shape["gy"])

    def on_device(grid_field, spectral_weight, conv_near, conv_far, mix_logits, channel_bias):
        _, channels, local_rows, local_cols = grid_field.shape
        layers = spectral_weight.shape[0]
        share = spectral_weight.shape[-1]
        devices = sizes[0] * sizes[1]
        cells_x, cells_y = local_rows * sizes[0], local_cols * sizes[1]
        modes_x = share * devices // MODES_Y
        per_share = max(share // MODES_Y, 1)
        blocks = modes_x // per_share
        groups = local_rows // GROUP
        planes = local_cols // LANES
        assert share * per_share in (16, 32, 128)
        assert groups * GROUP == local_rows and 8 * groups <= LANES and groups >= 4
        assert groups % 4 == 0
        assert cells_x % 4 == 0 and cells_y % 4 == 0
        assert planes * LANES == local_cols and planes in (1, 2, 4)

        mode = jnp.arange(2 * modes_x, dtype=jnp.int32)
        slot = mode % modes_x % blocks * per_share + mode % modes_x // blocks
        row_mode = jnp.where(slot < modes_x // 2, slot, slot + (cells_x - modes_x))
        turn = jnp.where(mode < modes_x, 0, 3 * cells_x // 4)
        index = jnp.arange(local_rows, dtype=jnp.int32)
        row_at = index // GROUP * GROUP + group_order(index % GROUP)
        row_at = row_at + lax.axis_index("gx") * local_rows
        phase = (row_mode[:, None] * row_at[None, :] + turn[:, None]) % cells_x
        rtab = jnp.cos(phase.astype(f32) * (full_turn / cells_x))

        index = jnp.arange(local_cols, dtype=jnp.int32)
        col_at = lax.axis_index("gy") * local_cols + natural_column(index, local_cols)
        mode = jnp.arange(2 * MODES_Y, dtype=jnp.int32)
        turn = jnp.where(mode < MODES_Y, 0, cells_y // 4)
        phase = ((mode % MODES_Y)[:, None] * col_at[None, :] + turn[:, None]) % cells_y
        ctab = jnp.cos(phase.astype(f32) * (full_turn / cells_y))

        field = main_call(
            grid_field[0],
            spectral_weight.transpose(0, 2, 3, 1, 4),
            conv_near.transpose(1, 0, 2),
            conv_far.transpose(1, 0, 2),
            rtab, ctab, mix_logits, channel_bias,
            sizes, cells_x * cells_y,
        )
        return restore_call(field, channels)[None]

    in_specs = (
        P(None, None, "gx", "gy"),
        P(None, None, None, None, ("gx", "gy")),
        P(),
        P(),
        P(),
        P(),
    )
    return jax.shard_map(
        on_device,
        mesh=mesh,
        in_specs=in_specs,
        out_specs=P(None, None, "gx", "gy"),
        check_vma=False,
    )
```
